256 devices in a mesh: chan: 4 (over x_hi, core), tm: 16 (over x_lo, z), stat: 4 (over y).
Axes of the slice: x: 4 (x_hi: 2, x_lo: 2; x = x_hi * 2 + x_lo), y: 4, z: 8, core: 2. Of those that a mesh axis runs over, the one named last changes fastest.
Arguments:
- voltages: bfloat16 [8, 2, 512, 32768], P('chan', None, 'stat', 'tm'), may hold values from -6 to 6
- ref_index: int32 [8], replicated, may hold values from 0 to 511
- positions: int32 [32768], P('tm'), may hold values from 0 to 255
- aperture_weight: float32 [256], replicated, may hold values from 0.25 to 4
Outputs:
- coefficients: float32 [512, 8, 8, 128], P(('stat', 'tm', 'chan'))
The draws below stay inside these ranges and needn't reach their ends.
Inputs may be any that keep to these rules, and one draw needn't show every extreme that they name: Each entry of ref_index is a station number; entries may repeat. Each entry of positions is a raster cell index of the 16 x 16 raster.
All inputs are finite; a program needn't handle non-finite values.
Results may differ from the reference program's by a relative error of at most 0.0003.
Values may be sent and summed in bfloat16 or wider, within the bound.
A program may use at most 128 MiB of HBM per device.

```python
import math
import jax
import jax.numpy as jnp
from jax import lax

STATIONS = 512
REFS = 8
RASTER = 16
ZERN = 64
TIME_DEV = 2048
CHANNELS = 8
TIME = 32768


def place_ends(array, rng, low, largest):
    longest = array.shape.index(max(array.shape))
    spots = []
    for shift in (0, 1):
        where = [jax.random.randint(jax.random.fold_in(rng, axis), (), 0, length) for axis, length in enumerate(array.shape)]
        where[longest] = (where[longest] + shift) % array.shape[longest]
        spots.append(tuple(where))
    return array.at[spots[0]].set(low).at[spots[1]].set(largest)


def spiked(result, rng, source, target, parts, factor):
    owner, partner = [(jnp.arange(result.shape[position]) // (result.shape[position] // parts)).reshape([-1 if axis == position else 1 for axis in range(result.ndim)]) for position in (source, target)]
    chosen = jax.random.permutation(rng, parts)[partner]
    strong = (owner == chosen) | (owner == (partner + parts // 2) % parts)
    return jnp.where(strong, factor * result, result)


def block_scale(own_key, dims, pieces, smallest, high):
    loudness, own = 1.0, jax.random.fold_in(own_key, 6)
    for axis_at, parts in pieces:
        heights = jnp.exp(jax.random.uniform(jax.random.fold_in(own, axis_at), (parts,), jnp.float32, smallest / len(pieces), high / len(pieces)))
        loudness = loudness * jnp.repeat(heights, dims[axis_at] // parts).reshape([-1 if axis == axis_at else 1 for axis in range(len(dims))])
    return loudness


def bell_draw_with(own_key, dims, scale, bound, cuts, heavy, held_as=jnp.bfloat16):
    values = scale * jax.random.normal(own_key, dims, jnp.float32)
    if cuts:
        values = values * block_scale(own_key, dims, cuts, -0.22, 0.18)
    return jnp.clip(spiked(values, jax.random.fold_in(own_key, 3), *heavy), -bound, bound).astype(held_as)


def setup_inputs(seed: int = 0) -> dict:
    streams_of = jax.random.split(jax.random.key(seed), 5)
    voltages = bell_draw_with(streams_of[0], (CHANNELS, 2, STATIONS, TIME), 1.0, 6.0, ((0, 4), (2, 4), (3, 16)), (3, 2, 16, 2.0))
    ref_index = place_ends(jax.random.randint(streams_of[1], (REFS,), 0, STATIONS), jax.random.fold_in(streams_of[1], 1), 0, STATIONS - 1).astype(jnp.int32)
    positions = place_ends(jax.random.randint(streams_of[2], (TIME,), 0, RASTER * RASTER), jax.random.fold_in(streams_of[2], 1), 0, (RASTER * RASTER) - 1).astype(jnp.int32)
    aperture_weight = jnp.clip(jnp.exp(jax.random.uniform(streams_of[3], (RASTER * RASTER,), jnp.float32, math.log(0.25), math.log(4.0))), 0.25, 4.0)
    return dict(voltages=voltages, ref_index=ref_index, positions=positions, aperture_weight=aperture_weight)


def zernike_table(raster, count):
    cell_ids = jnp.arange(raster * raster, dtype=jnp.int32)
    half_width = raster / 2.0
    grid_x = ((cell_ids // raster - raster // 2).astype(jnp.float32) + 0.5) / half_width
    grid_y = ((cell_ids % raster - raster // 2).astype(jnp.float32) + 0.5) / half_width
    radius_sq = grid_x * grid_x + grid_y * grid_y
    in_disk = jnp.where(radius_sq <= 1.0, 1.0, 0.0).astype(jnp.float32)
    columns = []
    degree = 0
    while len(columns) < count:
        for azimuth in range(-degree, degree + 1, 2):
            if len(columns) < count:
                order_abs = abs(azimuth)
                real_pow = jnp.ones_like(grid_x)
                imag_pow = jnp.zeros_like(grid_x)
                for power_i in range(order_abs):
                    real_pow, imag_pow = (real_pow * grid_x - imag_pow * grid_y, real_pow * grid_y + imag_pow * grid_x)
                radial = jnp.zeros_like(grid_x)
                for term_k in range((degree - order_abs) // 2 + 1):
                    weight_k = (-1) ** term_k * math.factorial(degree - term_k) / (math.factorial(term_k) * math.factorial((degree + order_abs) // 2 - term_k) * math.factorial((degree - order_abs) // 2 - term_k))
                    radial = radial + jnp.float32(weight_k) * radius_sq ** ((degree - 2 * term_k - order_abs) // 2)
                if azimuth > 0:
                    column = radial * real_pow * jnp.float32(math.sqrt(2.0 * (degree + 1)))
                elif azimuth < 0:
                    column = radial * imag_pow * jnp.float32(math.sqrt(2.0 * (degree + 1)))
                else:
                    column = radial * jnp.float32(math.sqrt(degree + 1.0))
                columns.append(column * in_disk)
        degree += 1
    return jnp.stack(columns, axis=1)

def dft_real():
    cell_ids = jnp.arange(RASTER * RASTER, dtype=jnp.int32)
    row_coord = cell_ids // RASTER - RASTER // 2
    col_coord = cell_ids % RASTER - RASTER // 2
    phases = (row_coord[:, None] * row_coord[None, :] + col_coord[:, None] * col_coord[None, :]) % RASTER
    angles = phases.astype(jnp.float32) * jnp.float32(2.0 * math.pi / RASTER)
    cosine = jnp.cos(angles)
    sine_part = jnp.sin(angles)
    upper_rows = jnp.concatenate([cosine, sine_part], axis=1)
    bottom = jnp.concatenate([-sine_part, cosine], axis=1)
    return jnp.concatenate([upper_rows, bottom], axis=0)

def fit_tables(aperture_weight):
    zernike = zernike_table(RASTER, ZERN)
    weighted = zernike * aperture_weight[:, None]
    gram_matrix = jnp.dot(zernike.T, weighted, precision=lax.Precision.HIGHEST)
    factor = jnp.linalg.cholesky(gram_matrix)
    return (weighted, factor)

def finish(beam, weighted, factor, dft_table):
    leading = beam.shape[:3]
    flat_maps = beam.reshape(leading + (2 * RASTER * RASTER,))
    aperture = jnp.dot(flat_maps, dft_table.T, precision=lax.Precision.HIGHEST)
    aperture = aperture.reshape(leading + (2, RASTER * RASTER))
    projected = jnp.dot(aperture, weighted, precision=lax.Precision.HIGHEST)
    stacked = projected.reshape(-1, ZERN).T
    solved = jax.scipy.linalg.cho_solve((factor, True), stacked)
    return solved.T.reshape(leading + (2 * ZERN,))

def reference(voltages, ref_index, positions, aperture_weight):
    references = voltages[:, :, ref_index, :]
    cells = RASTER * RASTER
    blocks = TIME // TIME_DEV

    def per_channel(pair):
        volt, refs = pair

        def step(total, index):
            begin = index * TIME_DEV
            volt_blk = lax.dynamic_slice_in_dim(volt, begin, TIME_DEV, 2).astype(jnp.float32)
            ref_blk = lax.dynamic_slice_in_dim(refs, begin, TIME_DEV, 2).astype(jnp.float32)
            pos_blk = lax.dynamic_slice_in_dim(positions, begin, TIME_DEV, 0)
            real_part = ref_blk[0][:, None, :] * volt_blk[0][None] + ref_blk[1][:, None, :] * volt_blk[1][None]
            imag_part = ref_blk[0][:, None, :] * volt_blk[1][None] - ref_blk[1][:, None, :] * volt_blk[0][None]
            rows = jnp.stack([real_part, imag_part], axis=1)
            rows = jnp.moveaxis(rows, 3, 0).reshape(TIME_DEV, -1)
            return (total + jax.ops.segment_sum(rows, pos_blk, num_segments=cells), None)
        start_total = jnp.zeros((cells, REFS * 2 * STATIONS), jnp.float32)
        total, unused = lax.scan(step, start_total, jnp.arange(blocks, dtype=jnp.int32))
        return total
    sums = lax.map(per_channel, (voltages, references))
    beam = sums.reshape(CHANNELS, cells, REFS, 2, STATIONS)
    scale = (TIME / cells) ** (-0.5)
    beam = jnp.transpose(beam, (4, 0, 2, 3, 1)) * scale
    weighted, factor = fit_tables(aperture_weight)
    return finish(beam, weighted, factor, dft_real())
```

```python
import functools
import math

import jax
import jax.numpy as jnp
import numpy as np
from jax import lax
from jax.experimental import pallas as pl
from jax.experimental.pallas import tpu as pltpu
from jax.sharding import PartitionSpec as P

RASTER = 16
CELLS = RASTER * RASTER
ZERN = 64
REFS = 8
MESH = pl.DeviceIdType.MESH
F32 = jnp.float32
BF16 = jnp.bfloat16
HIGHEST = lax.Precision.HIGHEST
NT = (((1,), (1,)), ((), ()))


def zernike_table():
    cells = np.arange(CELLS)
    x = (cells // RASTER - RASTER // 2 + 0.5) / (RASTER / 2.0)
    y = (cells % RASTER - RASTER // 2 + 0.5) / (RASTER / 2.0)
    radius_sq = x * x + y * y
    rows = []
    degree = 0
    while len(rows) < ZERN:
        for azimuth in range(-degree, degree + 1, 2):
            if len(rows) == ZERN:
                break
            order = abs(azimuth)
            power = (x + 1j * y) ** order
            radial = np.zeros_like(x)
            for k in range((degree - order) // 2 + 1):
                weight = (-1) ** k * math.factorial(degree - k)
                weight /= math.factorial(k)
                weight /= math.factorial((degree + order) // 2 - k)
                weight /= math.factorial((degree - order) // 2 - k)
                radial = radial + weight * radius_sq ** ((degree - 2 * k - order) // 2)
            if azimuth > 0:
                row = radial * power.real * math.sqrt(2.0 * (degree + 1))
            elif azimuth < 0:
                row = radial * power.imag * math.sqrt(2.0 * (degree + 1))
            else:
                row = radial * math.sqrt(degree + 1.0)
            rows.append(np.where(radius_sq <= 1.0, row, 0.0))
        degree += 1
    return np.stack(rows).astype(np.float32)


def dft_table(scale):
    cells = np.arange(CELLS)
    a = cells // RASTER - RASTER // 2
    b = cells % RASTER - RASTER // 2
    phases = (a[:, None] * a[None, :] + b[:, None] * b[None, :]) % RASTER
    angles = phases * (2.0 * math.pi / RASTER)
    both = np.concatenate([np.cos(angles), -np.sin(angles)], axis=1)
    return (both * scale).astype(np.float32)


def fit_operator(zern, weight, dft):
    weighted = zern * weight
    gram = lax.dot_general(weighted, zern, NT, precision=HIGHEST, preferred_element_type=F32)
    rows = lax.broadcasted_iota(jnp.int32, (ZERN, ZERN), 0)
    cols = lax.broadcasted_iota(jnp.int32, (ZERN, ZERN), 1)
    both = jnp.concatenate([gram, (rows == cols).astype(F32)], axis=1)
    row_ids = lax.broadcasted_iota(jnp.int32, (ZERN, 2 * ZERN), 0)
    for k in range(ZERN):
        pivot_row = both[k : k + 1, :] * (1.0 / both[k : k + 1, k : k + 1])
        reduced = both - both[:, k : k + 1] * pivot_row
        both = jnp.where(row_ids == k, pivot_row, reduced)
    padded = jnp.concatenate([jnp.zeros_like(weighted), weighted], axis=0)
    solve = jnp.dot(both, padded, precision=HIGHEST, preferred_element_type=F32)
    return jnp.dot(solve, dft, precision=HIGHEST, preferred_element_type=F32)


def exchange_kernel(
    volt_ref, index_ref, zern_ref, weight_ref, dft_ref, out_ref, table_ref,
    own, got, send_sem, recv_sem,
):
    n = lax.axis_size("stat")
    me = lax.axis_index("stat")
    chans, parts, stations, times = volt_ref.shape
    barrier = pltpu.get_barrier_semaphore()
    for d in range(1, n):
        pl.semaphore_signal(
            barrier, inc=1, device_id={"stat": lax.rem(me + d, n)}, device_id_type=MESH
        )
    cols = lax.broadcasted_iota(jnp.int32, (2 * REFS, parts * stations), 1)
    rows = lax.broadcasted_iota(jnp.int32, (2 * REFS, parts * stations), 0)
    wanted = index_ref[...] - me * stations
    inside = (wanted >= 0) & (wanted < stations)
    target = jnp.where(inside, wanted, -parts * stations) + (rows // REFS) * stations
    select = jnp.where(cols == target, 1.0, 0.0).astype(BF16)
    for c in range(chans):
        block = volt_ref[c].reshape(parts * stations, times)
        own[c] = jnp.dot(select, block, preferred_element_type=F32).astype(BF16)
    pl.semaphore_wait(barrier, n - 1)
    copies = []
    for d in range(1, n):
        copy = pltpu.make_async_remote_copy(
            src_ref=own, dst_ref=got.at[d - 1], send_sem=send_sem.at[d - 1],
            recv_sem=recv_sem.at[d - 1], device_id={"stat": lax.rem(me + d, n)},
            device_id_type=MESH,
        )
        copy.start()
        copies.append(copy)
    operator = fit_operator(zern_ref[...], weight_ref[...], dft_ref[...])
    table = jnp.concatenate([operator[:, :CELLS], operator[:, CELLS:]], axis=0)
    high = table.astype(BF16)
    table_ref[: 2 * ZERN, :] = high
    table_ref[2 * ZERN :, :] = (table - high.astype(F32)).astype(BF16)
    for copy in copies:
        copy.wait()
    for c in range(chans):
        total = own[c].astype(F32)
        for d in range(1, n):
            total = total + got[d - 1, c].astype(F32)
        out_ref[c] = total


def correlate_kernel(volt_ref, refs_ref, pos_ref, table_ref, part_ref, field, left_a, left_b):
    chans, parts, stations, times = volt_ref.shape
    step = 512
    for t in range(0, times, step):
        cells = lax.broadcasted_iota(jnp.int32, (CELLS, step), 0)
        onehot = jnp.where(cells == pos_ref[:, t : t + step], 1.0, 0.0).astype(BF16)
        both = jnp.dot(table_ref[...], onehot, preferred_element_type=F32)
        field[:, t : t + step] = both[: 2 * ZERN] + both[2 * ZERN :]
    lane = lax.broadcasted_iota(jnp.int32, (stations, 2 * ZERN), 1)
    rows, width = 16, 256

    def build(left, c, r):
        for t in range(0, times, width):
            at = slice(t, t + width)
            re = jnp.broadcast_to(refs_ref[c, pl.ds(r, 1), at], (rows, width))
            im = jnp.broadcast_to(refs_ref[c, pl.ds(r + REFS, 1), at], (rows, width))
            for j in range(0, ZERN, rows):
                h = field[j : j + rows, at]
                g = field[ZERN + j : ZERN + j + rows, at]
                for base, value in ((j, re * h + im * g), (ZERN + j, re * g - im * h)):
                    high = value.astype(BF16)
                    left[base : base + rows, at] = high
                    low = (value - high.astype(F32)).astype(BF16)
                    left[2 * ZERN + base : 2 * ZERN + base + rows, at] = low

    def multiply(left, c, r):
        block = volt_ref[c].reshape(parts * stations, times)
        both = lax.dot_general(block, left[...], NT, preferred_element_type=F32)
        both = both[:, : 2 * ZERN] + both[:, 2 * ZERN :]
        real, imag = both[:stations], pltpu.roll(both[stations:], ZERN, 1)
        out = real + jnp.where(lane < ZERN, -imag, imag)
        part_ref[pl.ds(c * REFS + r, stations, stride=chans * REFS), :] = out

    build(left_a, 0, 0)
    for c in range(chans):

        def body(i, carry, c=c):
            r = 2 * i
            build(left_b, c, r + 1)
            multiply(left_a, c, r)
            follow = r + 2
            wrap = follow == REFS
            build(left_a, jnp.where(wrap, min(c + 1, chans - 1), c), jnp.where(wrap, 0, follow))
            multiply(left_b, c, r + 1)
            return carry

        lax.fori_loop(0, REFS // 2, body, 0)


def regroup_kernel(part_ref, out_ref, side, held, got, side_send, side_recv, send_sem, recv_sem):
    tm, q = lax.axis_index("tm"), lax.axis_index("chan")
    n_tm, n_q = lax.axis_size("tm"), lax.axis_size("chan")
    n_z = n_tm // 2
    x, z = tm // n_z, lax.rem(tm, n_z)
    other = 1 - x
    chunk = part_ref.shape[0] // (n_tm * n_q)
    group = chunk * n_q
    half = group * n_z
    barrier = pltpu.get_barrier_semaphore()
    partner = {"tm": other * n_z + z}
    pl.semaphore_signal(barrier, inc=1, device_id=partner, device_id_type=MESH)

    def peer(dz, dq):
        return {"tm": x * n_z + lax.rem(z + dz, n_z), "chan": lax.rem(q + dq, n_q)}

    order = sorted(range(n_z), key=lambda d: -min(d, n_z - d))
    pairs = [(dz, dq) for dz in order for dq in range(n_q) if dz or dq]
    for dz, dq in pairs:
        pl.semaphore_signal(barrier, inc=1, device_id=peer(dz, dq), device_id_type=MESH)
    pl.semaphore_wait(barrier, len(pairs) + 1)

    across = []
    for k, dz in enumerate(order):
        to = lax.rem(z + dz, n_z)
        copy = pltpu.make_async_remote_copy(
            src_ref=part_ref.at[pl.ds(pl.multiple_of(other * half + to * group, group), group)],
            dst_ref=side.at[k], send_sem=side_send.at[k], recv_sem=side_recv.at[k],
            device_id=partner, device_id_type=MESH,
        )
        copy.start()
        across.append(copy)
    copies = []
    for k, dz in enumerate(order):
        across[k].wait_recv()
        to = lax.rem(z + dz, n_z)
        mine = part_ref[pl.ds(pl.multiple_of(x * half + to * group, group), group)]
        held[k] = mine + side[k]
        for dq in range(n_q):
            if not (dz or dq):
                continue
            slot = dz * n_q + dq
            aim = lax.rem(q + dq, n_q)
            copy = pltpu.make_async_remote_copy(
                src_ref=held.at[k, pl.ds(pl.multiple_of(aim * chunk, chunk), chunk)],
                dst_ref=got.at[slot], send_sem=send_sem.at[slot], recv_sem=recv_sem.at[slot],
                device_id=peer(dz, dq), device_id_type=MESH,
            )
            copy.start()
            copies.append(copy)
    for copy in copies:
        copy.wait_recv()
    stations = out_ref.shape[0]
    rows = chunk // stations
    for dq in range(n_q):
        total = None
        for dz in range(n_z):
            if dz or dq:
                term = got[dz * n_q + dq]
            else:
                term = held[n_z - 1, pl.ds(pl.multiple_of(q * chunk, chunk), chunk)]
            total = term if total is None else total + term
        origin = lax.rem(q - dq + n_q, n_q)
        for s in range(stations):
            out_ref[s, pl.ds(pl.multiple_of(origin * rows, rows), rows)] = total[
                s * rows : (s + 1) * rows
            ]
    for copy in across + copies:
        copy.wait_send()


def on_device(voltages, ref_index, positions, aperture_weight):
    chans, parts, stations, times = voltages.shape
    n_stat, n_tm, n_q = lax.axis_size("stat"), lax.axis_size("tm"), lax.axis_size("chan")
    scale = (n_tm * times / CELLS) ** (-0.5)
    zern = jnp.asarray(zernike_table())
    dft = jnp.asarray(dft_table(scale))
    index = jnp.tile(ref_index, 2)[:, None]
    vmem = pl.BlockSpec(memory_space=pltpu.VMEM)
    dma = pltpu.SemaphoreType.DMA
    refs, table = pl.pallas_call(
        exchange_kernel,
        out_shape=(
            jax.ShapeDtypeStruct((chans, 2 * REFS, times), F32),
            jax.ShapeDtypeStruct((4 * ZERN, CELLS), BF16),
        ),
        in_specs=[vmem] * 5,
        out_specs=(vmem, vmem),
        scratch_shapes=[
            pltpu.VMEM((chans, 2 * REFS, times), BF16),
            pltpu.VMEM((n_stat - 1, chans, 2 * REFS, times), BF16),
            dma((n_stat - 1,)),
            dma((n_stat - 1,)),
        ],
        compiler_params=pltpu.CompilerParams(collective_id=0, has_side_effects=True),
        name="exchange",
    )(voltages, index, zern, aperture_weight[None, :], dft)
    part = pl.pallas_call(
        correlate_kernel,
        out_shape=jax.ShapeDtypeStruct((stations * chans * REFS, 2 * ZERN), F32),
        in_specs=[vmem] * 4,
        out_specs=vmem,
        scratch_shapes=[
            pltpu.VMEM((2 * ZERN, times), F32),
            pltpu.VMEM((4 * ZERN, times), BF16),
            pltpu.VMEM((4 * ZERN, times), BF16),
        ],
        name="correlate",
    )(voltages, refs, positions[None, :], table)
    n_z = n_tm // 2
    rows = stations * chans * REFS
    chunk = rows // (n_tm * n_q)
    own = stations // (n_tm * n_q)
    out = pl.pallas_call(
        regroup_kernel,
        out_shape=jax.ShapeDtypeStruct((own, n_q * chans * REFS, 2 * ZERN), F32),
        in_specs=[vmem],
        out_specs=vmem,
        scratch_shapes=[
            pltpu.VMEM((n_z, chunk * n_q, 2 * ZERN), F32),
            pltpu.VMEM((n_z, chunk * n_q, 2 * ZERN), F32),
            pltpu.VMEM((n_z * n_q, chunk, 2 * ZERN), F32),
            dma((n_z,)),
            dma((n_z,)),
            dma((n_z * n_q,)),
            dma((n_z * n_q,)),
        ],
        compiler_params=pltpu.CompilerParams(collective_id=1, has_side_effects=True),
        name="regroup",
    )(part)
    return out.reshape(own, n_q * chans, REFS, 2 * ZERN)


def solution(mesh):
    in_specs = (P("chan", None, "stat", "tm"), P(), P("tm"), P())
    out_specs = P(("stat", "tm", "chan"), None, None, None)
    return jax.shard_map(
        on_device, mesh=mesh, in_specs=in_specs, out_specs=out_specs, check_vma=False
    )
```

```python
import functools
import math

import jax
import jax.numpy as jnp
import numpy as np
from jax import lax
from jax.experimental import pallas as pl
from jax.experimental.pallas import tpu as pltpu
from jax.sharding import PartitionSpec as P

RASTER = 16
CELLS = RASTER * RASTER
ZERN = 64
REFS = 8
MESH = pl.DeviceIdType.MESH
F32 = jnp.float32
BF16 = jnp.bfloat16
HIGHEST = lax.Precision.HIGHEST
NT = (((1,), (1,)), ((), ()))


def zernike_table():
    cells = np.arange(CELLS)
    x = (cells // RASTER - RASTER // 2 + 0.5) / (RASTER / 2.0)
    y = (cells % RASTER - RASTER // 2 + 0.5) / (RASTER / 2.0)
    radius_sq = x * x + y * y
    rows = []
    degree = 0
    while len(rows) < ZERN:
        for azimuth in range(-degree, degree + 1, 2):
            if len(rows) == ZERN:
                break
            order = abs(azimuth)
            power = (x + 1j * y) ** order
            radial = np.zeros_like(x)
            for k in range((degree - order) // 2 + 1):
                weight = (-1) ** k * math.factorial(degree - k)
                weight /= math.factorial(k)
                weight /= math.factorial((degree + order) // 2 - k)
                weight /= math.factorial((degree - order) // 2 - k)
                radial = radial + weight * radius_sq ** ((degree - 2 * k - order) // 2)
            if azimuth > 0:
                row = radial * power.real * math.sqrt(2.0 * (degree + 1))
            elif azimuth < 0:
                row = radial * power.imag * math.sqrt(2.0 * (degree + 1))
            else:
                row = radial * math.sqrt(degree + 1.0)
            rows.append(np.where(radius_sq <= 1.0, row, 0.0))
        degree += 1
    return np.stack(rows).astype(np.float32)


def dft_table(scale):
    cells = np.arange(CELLS)
    a = cells // RASTER - RASTER // 2
    b = cells % RASTER - RASTER // 2
    phases = (a[:, None] * a[None, :] + b[:, None] * b[None, :]) % RASTER
    angles = phases * (2.0 * math.pi / RASTER)
    both = np.concatenate([np.cos(angles), -np.sin(angles)], axis=1)
    return (both * scale).astype(np.float32)


def fit_operator(zern, weight, dft):
    weighted = zern * weight
    gram = lax.dot_general(weighted, zern, NT, precision=HIGHEST, preferred_element_type=F32)
    rows = lax.broadcasted_iota(jnp.int32, (ZERN, ZERN), 0)
    cols = lax.broadcasted_iota(jnp.int32, (ZERN, ZERN), 1)
    both = jnp.concatenate([gram, (rows == cols).astype(F32)], axis=1)
    row_ids = lax.broadcasted_iota(jnp.int32, (ZERN, 2 * ZERN), 0)
    for k in range(ZERN):
        pivot_row = both[k : k + 1, :] * (1.0 / both[k : k + 1, k : k + 1])
        reduced = both - both[:, k : k + 1] * pivot_row
        both = jnp.where(row_ids == k, pivot_row, reduced)
    padded = jnp.concatenate([jnp.zeros_like(weighted), weighted], axis=0)
    solve = jnp.dot(both, padded, precision=HIGHEST, preferred_element_type=F32)
    return jnp.dot(solve, dft, precision=HIGHEST, preferred_element_type=F32)


def exchange_kernel(
    volt_ref, index_ref, zern_ref, weight_ref, dft_ref, out_ref, table_ref,
    own, got, send_sem, recv_sem,
):
    n = lax.axis_size("stat")
    me = lax.axis_index("stat")
    chans, parts, stations, times = volt_ref.shape
    right, left = lax.rem(me + 1, n), lax.rem(me + n - 1, n)
    barrier = pltpu.get_barrier_semaphore()
    for peer in (right, left):
        pl.semaphore_signal(barrier, inc=1, device_id={"stat": peer}, device_id_type=MESH)
    cols = lax.broadcasted_iota(jnp.int32, (2 * REFS, parts * stations), 1)
    rows = lax.broadcasted_iota(jnp.int32, (2 * REFS, parts * stations), 0)
    wanted = jnp.zeros_like(rows)
    for r in range(REFS):
        wanted = jnp.where(lax.rem(rows, REFS) == r, index_ref[r], wanted)
    wanted = wanted - me * stations
    inside = (wanted >= 0) & (wanted < stations)
    target = jnp.where(inside, wanted, -parts * stations) + (rows // REFS) * stations
    select = jnp.where(cols == target, 1.0, 0.0).astype(BF16)
    for c in range(chans):
        block = volt_ref[c].reshape(parts * stations, times)
        own[c] = jnp.dot(select, block, preferred_element_type=F32).astype(BF16)
    pl.semaphore_wait(barrier, 2)

    def send(src, slot, c, peer):
        copy = pltpu.make_async_remote_copy(
            src_ref=src, dst_ref=got.at[slot, c], send_sem=send_sem.at[slot, c],
            recv_sem=recv_sem.at[slot, c], device_id={"stat": peer}, device_id_type=MESH,
        )
        copy.start()
        return copy

    copies = {}
    for c in range(chans):
        copies[0, c] = send(own.at[c], 0, c, right)
        copies[1, chans - 1 - c] = send(own.at[chans - 1 - c], 1, chans - 1 - c, left)
    copies[0, 0].wait_recv()
    copies[2, 0] = send(got.at[0, 0], 2, 0, right)
    copies[1, 1].wait_recv()
    copies[2, 1] = send(got.at[1, 1], 2, 1, left)
    operator = fit_operator(zern_ref[...], weight_ref[...], dft_ref[...])
    table = jnp.concatenate([operator[:, :CELLS], operator[:, CELLS:]], axis=0)
    high = table.astype(BF16)
    table_ref[: 2 * ZERN, :] = high
    table_ref[2 * ZERN :, :] = (table - high.astype(F32)).astype(BF16)
    for slot, c in ((0, 1), (1, 0), (2, 0), (2, 1)):
        copies[slot, c].wait_recv()
    for c in range(chans):
        total = own[c].astype(F32)
        for slot in range(3):
            total = total + got[slot, c].astype(F32)
        out_ref[c] = total
    for copy in copies.values():
        copy.wait_send()


def correlate_kernel(
    volt_ref, refs_ref, pos_ref, table_ref, out_ref, field, left_a, left_b,
    part, side, held, got, summed, last, side_send, side_recv, send_sem, recv_sem,
    last_send, last_recv,
):
    tm, q = lax.axis_index("tm"), lax.axis_index("chan")
    n_tm, n_q = lax.axis_size("tm"), lax.axis_size("chan")
    n_z = n_tm // 2
    x, z = tm // n_z, lax.rem(tm, n_z)
    other = 1 - x
    barrier = pltpu.get_barrier_semaphore()
    partner = {"tm": other * n_z + z}
    along = {d: {"tm": x * n_z + lax.rem(z + d, n_z)} for d in range(1, n_z)}
    across = {d: {"chan": lax.rem(q + d, n_q)} for d in range(1, n_q)}
    peers = [partner, *along.values(), *across.values()]
    for peer in peers:
        pl.semaphore_signal(barrier, inc=1, device_id=peer, device_id_type=MESH)
    chans, parts, stations, times = volt_ref.shape
    step = 512
    for t in range(0, times, step):
        cells = lax.broadcasted_iota(jnp.int32, (CELLS, step), 0)
        onehot = jnp.where(cells == pos_ref[:, t : t + step], 1.0, 0.0).astype(BF16)
        both = jnp.dot(table_ref[...], onehot, preferred_element_type=F32)
        field[:, t : t + step] = both[: 2 * ZERN] + both[2 * ZERN :]
    lane = lax.broadcasted_iota(jnp.int32, (stations, 2 * ZERN), 1)
    rows, width = 16, 256

    def build(left, c, r):
        for t in range(0, times, width):
            at = slice(t, t + width)
            re = jnp.broadcast_to(refs_ref[c, pl.ds(r, 1), at], (rows, width))
            im = jnp.broadcast_to(refs_ref[c, pl.ds(r + REFS, 1), at], (rows, width))
            for j in range(0, ZERN, rows):
                h = field[j : j + rows, at]
                g = field[ZERN + j : ZERN + j + rows, at]
                for base, value in ((j, re * h + im * g), (ZERN + j, re * g - im * h)):
                    high = value.astype(BF16)
                    left[base : base + rows, at] = high
                    low = (value - high.astype(F32)).astype(BF16)
                    left[2 * ZERN + base : 2 * ZERN + base + rows, at] = low

    def multiply(left, c, r):
        block = volt_ref[c].reshape(parts * stations, times)
        both = lax.dot_general(block, left[...], NT, preferred_element_type=F32)
        both = both[:, : 2 * ZERN] + both[:, 2 * ZERN :]
        real, imag = both[:stations], pltpu.roll(both[stations:], ZERN, 1)
        out = real + jnp.where(lane < ZERN, -imag, imag)
        part[c, pl.ds(r, stations, stride=REFS), :] = out

    def run(c, first, stop):
        def body(i, carry):
            r = 2 * i
            build(left_b, c, r + 1)
            multiply(left_a, c, r)
            follow = r + 2
            wrap = follow == REFS
            build(left_a, jnp.where(wrap, min(c + 1, chans - 1), c), jnp.where(wrap, 0, follow))
            multiply(left_b, c, r + 1)
            return carry

        lax.fori_loop(first, stop, body, 0)

    own = stations // (n_tm * n_q)
    chunk = own * REFS
    group = chunk * n_q
    order = sorted(range(n_z), key=lambda d: -min(d, n_z - d))

    def block(side_x, dz):
        start = (side_x * n_z + lax.rem(z + dz, n_z)) * group
        return pl.ds(pl.multiple_of(start, group), group)

    def send(src, dst, send, recv, peer):
        copy = pltpu.make_async_remote_copy(
            src_ref=src, dst_ref=dst, send_sem=send, recv_sem=recv,
            device_id=peer, device_id_type=MESH,
        )
        copy.start()
        return copy

    over, copies, final = {}, {}, {}

    def swap(c):
        for k, dz in enumerate(order):
            over[c, k] = send(
                part.at[c, block(other, dz)], side.at[c, k], side_send.at[c, k],
                side_recv.at[c, k], partner,
            )

    def forward(c, k):
        dz = order[k]
        over[c, k].wait_recv()
        held[c, k] = part[c, block(x, dz)] + side[c, k]
        if dz:
            copies[c, k] = send(
                held.at[c, k], got.at[c, k], send_sem.at[c, k], recv_sem.at[c, k], along[dz]
            )

    def reduce(c):
        total = held[c, n_z - 1]
        for k in range(n_z - 1):
            copies[c, k].wait_recv()
            total = total + got[c, k]
        summed[c] = total
        for d in range(1, n_q):
            aim = pl.multiple_of(lax.rem(q + d, n_q) * chunk, chunk)
            final[c, d] = send(
                summed.at[c, pl.ds(aim, chunk)], last.at[c, d - 1], last_send.at[c, d - 1],
                last_recv.at[c, d - 1], across[d],
            )

    def place(c, d, rows):
        origin = lax.rem(q - d + n_q, n_q)
        at = pl.ds(pl.multiple_of((origin * chans + c) * REFS, REFS), REFS)
        for s in range(own):
            out_ref[s, at] = rows[s * REFS : (s + 1) * REFS]

    build(left_a, 0, 0)
    run(0, 0, REFS // 2)
    pl.semaphore_wait(barrier, len(peers))
    swap(0)
    run(1, 0, REFS // 4)
    forward(0, 0)
    run(1, REFS // 4, REFS // 2)
    swap(1)
    for k in range(1, n_z):
        forward(0, k)
    for k in range(n_z - 2):
        forward(1, k)
    reduce(0)
    for k in range(n_z - 2, n_z):
        forward(1, k)
    reduce(1)
    for c in range(chans):
        place(c, 0, summed[c, pl.ds(pl.multiple_of(q * chunk, chunk), chunk)])
    for (c, d), copy in final.items():
        copy.wait_recv()
        place(c, d, last[c, d - 1])
    for copy in (*over.values(), *copies.values(), *final.values()):
        copy.wait_send()


def on_device(voltages, ref_index, positions, aperture_weight):
    chans, parts, stations, times = voltages.shape
    n_stat, n_tm, n_q = lax.axis_size("stat"), lax.axis_size("tm"), lax.axis_size("chan")
    scale = (n_tm * times / CELLS) ** (-0.5)
    zern = jnp.asarray(zernike_table())
    dft = jnp.asarray(dft_table(scale))
    vmem = pl.BlockSpec(memory_space=pltpu.VMEM)
    dma = pltpu.SemaphoreType.DMA
    refs, table = pl.pallas_call(
        exchange_kernel,
        out_shape=(
            jax.ShapeDtypeStruct((chans, 2 * REFS, times), F32),
            jax.ShapeDtypeStruct((4 * ZERN, CELLS), BF16),
        ),
        in_specs=[vmem, pl.BlockSpec(memory_space=pltpu.SMEM), vmem, vmem, vmem],
        out_specs=(vmem, vmem),
        scratch_shapes=[
            pltpu.VMEM((chans, 2 * REFS, times), BF16),
            pltpu.VMEM((n_stat - 1, chans, 2 * REFS, times), BF16),
            dma((n_stat - 1, chans)),
            dma((n_stat - 1, chans)),
        ],
        compiler_params=pltpu.CompilerParams(collective_id=0, has_side_effects=True),
        name="exchange",
    )(voltages, ref_index, zern, aperture_weight[None, :], dft)
    n_z = n_tm // 2
    own = stations // (n_tm * n_q)
    group = n_q * own * REFS
    wide = 2 * ZERN
    out = pl.pallas_call(
        correlate_kernel,
        out_shape=jax.ShapeDtypeStruct((own, n_q * chans * REFS, wide), F32),
        in_specs=[vmem] * 4,
        out_specs=vmem,
        scratch_shapes=[
            pltpu.VMEM((wide, times), F32),
            pltpu.VMEM((2 * wide, times), BF16),
            pltpu.VMEM((2 * wide, times), BF16),
            pltpu.VMEM((chans, stations * REFS, wide), F32),
            pltpu.VMEM((chans, n_z, group, wide), F32),
            pltpu.VMEM((chans, n_z, group, wide), F32),
            pltpu.VMEM((chans, n_z - 1, group, wide), F32),
            pltpu.VMEM((chans, group, wide), F32),
            pltpu.VMEM((chans, n_q - 1, own * REFS, wide), F32),
            dma((chans, n_z)),
            dma((chans, n_z)),
            dma((chans, n_z - 1)),
            dma((chans, n_z - 1)),
            dma((chans, n_q - 1)),
            dma((chans, n_q - 1)),
        ],
        compiler_params=pltpu.CompilerParams(collective_id=1, has_side_effects=True),
        name="correlate",
    )(voltages, refs, positions[None, :], table)
    return out.reshape(own, n_q * chans, REFS, 2 * ZERN)


def solution(mesh):
    in_specs = (P("chan", None, "stat", "tm"), P(), P("tm"), P())
    out_specs = P(("stat", "tm", "chan"), None, None, None)
    return jax.shard_map(
        on_device, mesh=mesh, in_specs=in_specs, out_specs=out_specs, check_vma=False
    )
```

```python
import functools
import math

import jax
import jax.numpy as jnp
import numpy as np
from jax import lax
from jax.experimental import pallas as pl
from jax.experimental.pallas import tpu as pltpu
from jax.sharding import PartitionSpec as P

RASTER = 16
CELLS = RASTER * RASTER
ZERN = 64
REFS = 8
MESH = pl.DeviceIdType.MESH
F32 = jnp.float32
BF16 = jnp.bfloat16
HIGHEST = lax.Precision.HIGHEST
NT = (((1,), (1,)), ((), ()))


def zernike_table():
    cells = np.arange(CELLS)
    x = (cells // RASTER - RASTER // 2 + 0.5) / (RASTER / 2.0)
    y = (cells % RASTER - RASTER // 2 + 0.5) / (RASTER / 2.0)
    radius_sq = x * x + y * y
    rows = []
    degree = 0
    while len(rows) < ZERN:
        for azimuth in range(-degree, degree + 1, 2):
            if len(rows) == ZERN:
                break
            order = abs(azimuth)
            power = (x + 1j * y) ** order
            radial = np.zeros_like(x)
            for k in range((degree - order) // 2 + 1):
                weight = (-1) ** k * math.factorial(degree - k)
                weight /= math.factorial(k)
                weight /= math.factorial((degree + order) // 2 - k)
                weight /= math.factorial((degree - order) // 2 - k)
                radial = radial + weight * radius_sq ** ((degree - 2 * k - order) // 2)
            if azimuth > 0:
                row = radial * power.real * math.sqrt(2.0 * (degree + 1))
            elif azimuth < 0:
                row = radial * power.imag * math.sqrt(2.0 * (degree + 1))
            else:
                row = radial * math.sqrt(degree + 1.0)
            rows.append(np.where(radius_sq <= 1.0, row, 0.0))
        degree += 1
    return np.stack(rows).astype(np.float32)


def dft_table(scale):
    cells = np.arange(CELLS)
    a = cells // RASTER - RASTER // 2
    b = cells % RASTER - RASTER // 2
    phases = (a[:, None] * a[None, :] + b[:, None] * b[None, :]) % RASTER
    angles = phases * (2.0 * math.pi / RASTER)
    both = np.concatenate([np.cos(angles), -np.sin(angles)], axis=1)
    return (both * scale).astype(np.float32)


def invert_gram(zern, weight):
    weighted = zern * weight
    gram = lax.dot_general(weighted, zern, NT, precision=HIGHEST, preferred_element_type=F32)
    rows = lax.broadcasted_iota(jnp.int32, (ZERN, ZERN), 0)
    cols = lax.broadcasted_iota(jnp.int32, (ZERN, ZERN), 1)
    both = jnp.concatenate([gram, (rows == cols).astype(F32)], axis=1)
    row_ids = lax.broadcasted_iota(jnp.int32, (ZERN, 2 * ZERN), 0)
    for k in range(ZERN):
        pivot_row = both[k : k + 1, :] * (1.0 / both[k : k + 1, k : k + 1])
        reduced = both - both[:, k : k + 1] * pivot_row
        both = jnp.where(row_ids == k, pivot_row, reduced)
    return weighted, both


def fit_operator(weighted, both, dft):
    padded = jnp.concatenate([jnp.zeros_like(weighted), weighted], axis=0)
    solve = jnp.dot(both, padded, precision=HIGHEST, preferred_element_type=F32)
    return jnp.dot(solve, dft, precision=HIGHEST, preferred_element_type=F32)


def exchange_kernel(
    volt_ref, index_ref, zern_ref, weight_ref, dft_ref, out_ref, table_ref,
    own, got, inverse_ref, send_sem, recv_sem,
):
    n = lax.axis_size("stat")
    me = lax.axis_index("stat")
    chans, parts, stations, times = volt_ref.shape
    right, left = lax.rem(me + 1, n), lax.rem(me + n - 1, n)
    barrier = pltpu.get_barrier_semaphore()
    for peer in (right, left):
        pl.semaphore_signal(barrier, inc=1, device_id={"stat": peer}, device_id_type=MESH)
    cols = lax.broadcasted_iota(jnp.int32, (2 * REFS, parts * stations), 1)
    rows = lax.broadcasted_iota(jnp.int32, (2 * REFS, parts * stations), 0)
    wanted = jnp.zeros_like(rows)
    for r in range(REFS):
        wanted = jnp.where(lax.rem(rows, REFS) == r, index_ref[r], wanted)
    wanted = wanted - me * stations
    inside = (wanted >= 0) & (wanted < stations)
    target = jnp.where(inside, wanted, -parts * stations) + (rows // REFS) * stations
    select = jnp.where(cols == target, 1.0, 0.0).astype(BF16)
    for c in range(chans):
        block = volt_ref[c].reshape(parts * stations, times)
        own[c] = jnp.dot(select, block, preferred_element_type=F32).astype(BF16)
    pl.semaphore_wait(barrier, 2)

    def send(src, slot, c, peer):
        copy = pltpu.make_async_remote_copy(
            src_ref=src, dst_ref=got.at[slot, c], send_sem=send_sem.at[slot, c],
            recv_sem=recv_sem.at[slot, c], device_id={"stat": peer}, device_id_type=MESH,
        )
        copy.start()
        return copy

    copies = {}
    for c in range(chans):
        copies[0, c] = send(own.at[c], 0, c, right)
        copies[1, chans - 1 - c] = send(own.at[chans - 1 - c], 1, chans - 1 - c, left)
    weighted, inverse = invert_gram(zern_ref[...], weight_ref[...])
    inverse_ref[...] = inverse
    copies[0, 0].wait_recv()
    copies[2, 0] = send(got.at[0, 0], 2, 0, right)
    copies[1, 1].wait_recv()
    copies[2, 1] = send(got.at[1, 1], 2, 1, left)
    operator = fit_operator(weighted, inverse_ref[...], dft_ref[...])
    table = jnp.concatenate([operator[:, :CELLS], operator[:, CELLS:]], axis=0)
    high = table.astype(BF16)
    table_ref[: 2 * ZERN, :] = high
    table_ref[2 * ZERN :, :] = (table - high.astype(F32)).astype(BF16)
    for slot, c in ((0, 1), (1, 0), (2, 0), (2, 1)):
        copies[slot, c].wait_recv()
    for c in range(chans):
        total = own[c].astype(F32)
        for slot in range(3):
            total = total + got[slot, c].astype(F32)
        out_ref[c] = total
    for copy in copies.values():
        copy.wait_send()


def correlate_kernel(
    volt_ref, refs_ref, pos_ref, table_ref, out_ref, field, left_a, left_b,
    part, side, held, got, summed, last, side_send, side_recv, send_sem, recv_sem,
    last_send, last_recv,
):
    tm, q = lax.axis_index("tm"), lax.axis_index("chan")
    n_tm, n_q = lax.axis_size("tm"), lax.axis_size("chan")
    n_z = n_tm // 2
    x, z = tm // n_z, lax.rem(tm, n_z)
    other = 1 - x
    barrier = pltpu.get_barrier_semaphore()
    partner = {"tm": other * n_z + z}
    along = {d: {"tm": x * n_z + lax.rem(z + d, n_z)} for d in range(1, n_z)}
    across = {d: {"chan": lax.rem(q + d, n_q)} for d in range(1, n_q)}
    peers = [partner, *along.values(), *across.values()]
    for peer in peers:
        pl.semaphore_signal(barrier, inc=1, device_id=peer, device_id_type=MESH)
    chans, parts, stations, times = volt_ref.shape
    step = 512
    for t in range(0, times, step):
        cells = lax.broadcasted_iota(jnp.int32, (CELLS, step), 0)
        onehot = jnp.where(cells == pos_ref[:, t : t + step], 1.0, 0.0).astype(BF16)
        both = jnp.dot(table_ref[...], onehot, preferred_element_type=F32)
        field[:, t : t + step] = both[: 2 * ZERN] + both[2 * ZERN :]
    lane = lax.broadcasted_iota(jnp.int32, (stations, 2 * ZERN), 1)
    rows, width = 16, 256

    def build(left, c, r):
        for t in range(0, times, width):
            at = slice(t, t + width)
            re = jnp.broadcast_to(refs_ref[c, pl.ds(r, 1), at], (rows, width))
            im = jnp.broadcast_to(refs_ref[c, pl.ds(r + REFS, 1), at], (rows, width))
            for j in range(0, ZERN, rows):
                h = field[j : j + rows, at]
                g = field[ZERN + j : ZERN + j + rows, at]
                for base, value in ((j, re * h + im * g), (ZERN + j, re * g - im * h)):
                    high = value.astype(BF16)
                    left[base : base + rows, at] = high
                    low = (value - high.astype(F32)).astype(BF16)
                    left[2 * ZERN + base : 2 * ZERN + base + rows, at] = low

    def multiply(left, c, r):
        block = volt_ref[c].reshape(parts * stations, times)
        both = lax.dot_general(block, left[...], NT, preferred_element_type=F32)
        both = both[:, : 2 * ZERN] + both[:, 2 * ZERN :]
        real, imag = both[:stations], pltpu.roll(both[stations:], ZERN, 1)
        out = real + jnp.where(lane < ZERN, -imag, imag)
        part[c, pl.ds(r, stations, stride=REFS), :] = out

    def run(c, first, stop):
        def body(i, carry):
            r = 2 * i
            build(left_b, c, r + 1)
            multiply(left_a, c, r)
            follow = r + 2
            wrap = follow == REFS
            build(left_a, jnp.where(wrap, min(c + 1, chans - 1), c), jnp.where(wrap, 0, follow))
            multiply(left_b, c, r + 1)
            return carry

        lax.fori_loop(first, stop, body, 0)

    own = stations // (n_tm * n_q)
    chunk = own * REFS
    group = chunk * n_q
    far = n_z // 2
    order = [far]
    for d in range(far - 1, 0, -1):
        order += [d, n_z - d]
    order.remove(far + 1)
    order.insert(4, far + 1)
    order.append(0)

    def block(side_x, dz):
        start = (side_x * n_z + lax.rem(z + dz, n_z)) * group
        return pl.ds(pl.multiple_of(start, group), group)

    def send(src, dst, send, recv, peer):
        copy = pltpu.make_async_remote_copy(
            src_ref=src, dst_ref=dst, send_sem=send, recv_sem=recv,
            device_id=peer, device_id_type=MESH,
        )
        copy.start()
        return copy

    over, copies, final = {}, {}, {}

    def swap(c):
        for k, dz in enumerate(order):
            over[c, k] = send(
                part.at[c, block(other, dz)], side.at[c, k], side_send.at[c, k],
                side_recv.at[c, k], partner,
            )

    def forward(c, k):
        dz = order[k]
        over[c, k].wait_recv()
        total = part[c, block(x, dz)] + side[c, k]
        if dz == far + 1:
            copies[c, 0].wait_recv()
            total = total + got[c, 0]
        held[c, k] = total
        if dz:
            copies[c, k] = send(
                held.at[c, k], got.at[c, k], send_sem.at[c, k], recv_sem.at[c, k],
                along[n_z - 1 if dz == far else dz],
            )

    def reduce(c):
        total = held[c, n_z - 1]
        for k in range(1, n_z - 1):
            copies[c, k].wait_recv()
            total = total + got[c, k]
        summed[c] = total
        for d in range(1, n_q):
            aim = pl.multiple_of(lax.rem(q + d, n_q) * chunk, chunk)
            final[c, d] = send(
                summed.at[c, pl.ds(aim, chunk)], last.at[c, d - 1], last_send.at[c, d - 1],
                last_recv.at[c, d - 1], across[d],
            )

    def place(c, d, rows):
        origin = lax.rem(q - d + n_q, n_q)
        at = pl.ds(pl.multiple_of((origin * chans + c) * REFS, REFS), REFS)
        for s in range(own):
            out_ref[s, at] = rows[s * REFS : (s + 1) * REFS]

    build(left_a, 0, 0)
    run(0, 0, REFS // 2)
    pl.semaphore_wait(barrier, len(peers))
    swap(0)
    run(1, 0, REFS // 4)
    forward(0, 0)
    run(1, REFS // 4, REFS // 2)
    swap(1)
    for k in range(1, n_z):
        forward(0, k)
    for k in range(n_z - 2):
        forward(1, k)
    reduce(0)
    for k in range(n_z - 2, n_z):
        forward(1, k)
    reduce(1)
    for c in range(chans):
        place(c, 0, summed[c, pl.ds(pl.multiple_of(q * chunk, chunk), chunk)])
    for (c, d), copy in final.items():
        copy.wait_recv()
        place(c, d, last[c, d - 1])
    for copy in (*over.values(), *copies.values(), *final.values()):
        copy.wait_send()


def on_device(voltages, ref_index, positions, aperture_weight):
    chans, parts, stations, times = voltages.shape
    n_stat, n_tm, n_q = lax.axis_size("stat"), lax.axis_size("tm"), lax.axis_size("chan")
    scale = (n_tm * times / CELLS) ** (-0.5)
    zern = jnp.asarray(zernike_table())
    dft = jnp.asarray(dft_table(scale))
    vmem = pl.BlockSpec(memory_space=pltpu.VMEM)
    dma = pltpu.SemaphoreType.DMA
    refs, table = pl.pallas_call(
        exchange_kernel,
        out_shape=(
            jax.ShapeDtypeStruct((chans, 2 * REFS, times), F32),
            jax.ShapeDtypeStruct((4 * ZERN, CELLS), BF16),
        ),
        in_specs=[vmem, pl.BlockSpec(memory_space=pltpu.SMEM), vmem, vmem, vmem],
        out_specs=(vmem, vmem),
        scratch_shapes=[
            pltpu.VMEM((chans, 2 * REFS, times), BF16),
            pltpu.VMEM((n_stat - 1, chans, 2 * REFS, times), BF16),
            pltpu.VMEM((ZERN, 2 * ZERN), F32),
            dma((n_stat - 1, chans)),
            dma((n_stat - 1, chans)),
        ],
        compiler_params=pltpu.CompilerParams(collective_id=0, has_side_effects=True),
        name="exchange",
    )(voltages, ref_index, zern, aperture_weight[None, :], dft)
    n_z = n_tm // 2
    own = stations // (n_tm * n_q)
    group = n_q * own * REFS
    wide = 2 * ZERN
    out = pl.pallas_call(
        correlate_kernel,
        out_shape=jax.ShapeDtypeStruct((own, n_q * chans * REFS, wide), F32),
        in_specs=[vmem] * 4,
        out_specs=vmem,
        scratch_shapes=[
            pltpu.VMEM((wide, times), F32),
            pltpu.VMEM((2 * wide, times), BF16),
            pltpu.VMEM((2 * wide, times), BF16),
            pltpu.VMEM((chans, stations * REFS, wide), F32),
            pltpu.VMEM((chans, n_z, group, wide), F32),
            pltpu.VMEM((chans, n_z, group, wide), F32),
            pltpu.VMEM((chans, n_z - 1, group, wide), F32),
            pltpu.VMEM((chans, group, wide), F32),
            pltpu.VMEM((chans, n_q - 1, own * REFS, wide), F32),
            dma((chans, n_z)),
            dma((chans, n_z)),
            dma((chans, n_z - 1)),
            dma((chans, n_z - 1)),
            dma((chans, n_q - 1)),
            dma((chans, n_q - 1)),
        ],
        compiler_params=pltpu.CompilerParams(collective_id=1, has_side_effects=True),
        name="correlate",
    )(voltages, refs, positions[None, :], table)
    return out.reshape(own, n_q * chans, REFS, 2 * ZERN)


def solution(mesh):
    in_specs = (P("chan", None, "stat", "tm"), P(), P("tm"), P())
    out_specs = P(("stat", "tm", "chan"), None, None, None)
    return jax.shard_map(
        on_device, mesh=mesh, in_specs=in_specs, out_specs=out_specs, check_vma=False
    )
```

```python
import functools
import math

import jax
import jax.numpy as jnp
import numpy as np
from jax import lax
from jax.experimental import pallas as pl
from jax.experimental.pallas import tpu as pltpu
from jax.sharding import PartitionSpec as P

RASTER = 16
CELLS = RASTER * RASTER
ZERN = 64
REFS = 8
MESH = pl.DeviceIdType.MESH
F32 = jnp.float32
BF16 = jnp.bfloat16
HIGHEST = lax.Precision.HIGHEST
NT = (((1,), (1,)), ((), ()))


def zernike_table():
    cells = np.arange(CELLS)
    x = (cells // RASTER - RASTER // 2 + 0.5) / (RASTER / 2.0)
    y = (cells % RASTER - RASTER // 2 + 0.5) / (RASTER / 2.0)
    radius_sq = x * x + y * y
    rows = []
    degree = 0
    while len(rows) < ZERN:
        for azimuth in range(-degree, degree + 1, 2):
            if len(rows) == ZERN:
                break
            order = abs(azimuth)
            power = (x + 1j * y) ** order
            radial = np.zeros_like(x)
            for k in range((degree - order) // 2 + 1):
                weight = (-1) ** k * math.factorial(degree - k)
                weight /= math.factorial(k)
                weight /= math.factorial((degree + order) // 2 - k)
                weight /= math.factorial((degree - order) // 2 - k)
                radial = radial + weight * radius_sq ** ((degree - 2 * k - order) // 2)
            if azimuth > 0:
                row = radial * power.real * math.sqrt(2.0 * (degree + 1))
            elif azimuth < 0:
                row = radial * power.imag * math.sqrt(2.0 * (degree + 1))
            else:
                row = radial * math.sqrt(degree + 1.0)
            rows.append(np.where(radius_sq <= 1.0, row, 0.0))
        degree += 1
    return np.stack(rows).astype(np.float32)


def dft_table(scale):
    cells = np.arange(CELLS)
    a = cells // RASTER - RASTER // 2
    b = cells % RASTER - RASTER // 2
    phases = (a[:, None] * a[None, :] + b[:, None] * b[None, :]) % RASTER
    angles = phases * (2.0 * math.pi / RASTER)
    both = np.concatenate([np.cos(angles), -np.sin(angles)], axis=1)
    return (both * scale).astype(np.float32)


def invert_gram(zern, weight):
    weighted = zern * weight
    gram = lax.dot_general(weighted, zern, NT, precision=HIGHEST, preferred_element_type=F32)
    rows = lax.broadcasted_iota(jnp.int32, (ZERN, ZERN), 0)
    cols = lax.broadcasted_iota(jnp.int32, (ZERN, ZERN), 1)
    both = jnp.concatenate([gram, (rows == cols).astype(F32)], axis=1)
    row_ids = lax.broadcasted_iota(jnp.int32, (ZERN, 2 * ZERN), 0)
    for k in range(ZERN):
        pivot_row = both[k : k + 1, :] * (1.0 / both[k : k + 1, k : k + 1])
        reduced = both - both[:, k : k + 1] * pivot_row
        both = jnp.where(row_ids == k, pivot_row, reduced)
    return weighted, both


def fit_operator(weighted, both, dft):
    padded = jnp.concatenate([jnp.zeros_like(weighted), weighted], axis=0)
    solve = jnp.dot(both, padded, precision=HIGHEST, preferred_element_type=F32)
    return jnp.dot(solve, dft, precision=HIGHEST, preferred_element_type=F32)


def exchange_kernel(
    volt_hbm, index_ref, zern_ref, weight_ref, dft_hbm, out_ref, table_ref,
    volt_ref, dft_ref, own, got, inverse_ref, load_sem, send_sem, recv_sem,
):
    n = lax.axis_size("stat")
    me = lax.axis_index("stat")
    chans, parts, stations, times = volt_ref.shape
    right, left = lax.rem(me + 1, n), lax.rem(me + n - 1, n)
    barrier = pltpu.get_barrier_semaphore()
    for peer in (right, left):
        pl.semaphore_signal(barrier, inc=1, device_id={"stat": peer}, device_id_type=MESH)
    loads = [
        pltpu.make_async_copy(volt_hbm.at[c], volt_ref.at[c], load_sem.at[c])
        for c in range(chans)
    ]
    loads.append(pltpu.make_async_copy(dft_hbm, dft_ref, load_sem.at[chans]))
    for load in loads:
        load.start()
    cols = lax.broadcasted_iota(jnp.int32, (2 * REFS, parts * stations), 1)
    rows = lax.broadcasted_iota(jnp.int32, (2 * REFS, parts * stations), 0)
    wanted = jnp.zeros_like(rows)
    for r in range(REFS):
        wanted = jnp.where(lax.rem(rows, REFS) == r, index_ref[r], wanted)
    wanted = wanted - me * stations
    inside = (wanted >= 0) & (wanted < stations)
    target = jnp.where(inside, wanted, -parts * stations) + (rows // REFS) * stations
    select = jnp.where(cols == target, 1.0, 0.0).astype(BF16)
    for c in range(chans):
        loads[c].wait()
        block = volt_ref[c].reshape(parts * stations, times)
        own[c] = jnp.dot(select, block, preferred_element_type=F32).astype(BF16)
    pl.semaphore_wait(barrier, 2)

    def send(src, slot, c, peer):
        copy = pltpu.make_async_remote_copy(
            src_ref=src, dst_ref=got.at[slot, c], send_sem=send_sem.at[slot, c],
            recv_sem=recv_sem.at[slot, c], device_id={"stat": peer}, device_id_type=MESH,
        )
        copy.start()
        return copy

    copies = {}
    for c in range(chans):
        copies[0, c] = send(own.at[c], 0, c, right)
        copies[1, chans - 1 - c] = send(own.at[chans - 1 - c], 1, chans - 1 - c, left)
    weighted, inverse = invert_gram(zern_ref[...], weight_ref[...])
    inverse_ref[...] = inverse
    copies[0, 0].wait_recv()
    copies[2, 0] = send(got.at[0, 0], 2, 0, right)
    copies[1, 1].wait_recv()
    copies[2, 1] = send(got.at[1, 1], 2, 1, left)
    loads[chans].wait()
    operator = fit_operator(weighted, inverse_ref[...], dft_ref[...])
    table = jnp.concatenate([operator[:, :CELLS], operator[:, CELLS:]], axis=0)
    high = table.astype(BF16)
    table_ref[: 2 * ZERN, :] = high
    table_ref[2 * ZERN :, :] = (table - high.astype(F32)).astype(BF16)
    for slot, c in ((0, 1), (1, 0), (2, 0), (2, 1)):
        copies[slot, c].wait_recv()
    for c in range(chans):
        total = own[c].astype(F32)
        for slot in range(3):
            total = total + got[slot, c].astype(F32)
        out_ref[c] = total
    for copy in copies.values():
        copy.wait_send()


def correlate_kernel(
    volt_hbm, refs_ref, pos_ref, table_ref, out_ref, volt_ref, field, left_a, left_b,
    part, side, held, got, summed, last, side_send, side_recv, send_sem, recv_sem,
    last_send, last_recv, load_sem,
):
    tm, q = lax.axis_index("tm"), lax.axis_index("chan")
    n_tm, n_q = lax.axis_size("tm"), lax.axis_size("chan")
    n_z = n_tm // 2
    x, z = tm // n_z, lax.rem(tm, n_z)
    other = 1 - x
    barrier = pltpu.get_barrier_semaphore()
    partner = {"tm": other * n_z + z}
    along = {d: {"tm": x * n_z + lax.rem(z + d, n_z)} for d in range(1, n_z)}
    across = {d: {"chan": lax.rem(q + d, n_q)} for d in range(1, n_q)}
    peers = [partner, *along.values(), *across.values()]
    for peer in peers:
        pl.semaphore_signal(barrier, inc=1, device_id=peer, device_id_type=MESH)
    chans, parts, stations, times = volt_ref.shape
    loads = [
        pltpu.make_async_copy(volt_hbm.at[c], volt_ref.at[c], load_sem.at[c])
        for c in range(chans)
    ]
    for load in loads:
        load.start()
    step = 512
    for t in range(0, times, step):
        cells = lax.broadcasted_iota(jnp.int32, (CELLS, step), 0)
        onehot = jnp.where(cells == pos_ref[:, t : t + step], 1.0, 0.0).astype(BF16)
        both = jnp.dot(table_ref[...], onehot, preferred_element_type=F32)
        field[:, t : t + step] = both[: 2 * ZERN] + both[2 * ZERN :]
    lane = lax.broadcasted_iota(jnp.int32, (stations, 2 * ZERN), 1)
    rows, width = 16, 256

    def build(left, c, r):
        for t in range(0, times, width):
            at = slice(t, t + width)
            re = jnp.broadcast_to(refs_ref[c, pl.ds(r, 1), at], (rows, width))
            im = jnp.broadcast_to(refs_ref[c, pl.ds(r + REFS, 1), at], (rows, width))
            for j in range(0, ZERN, rows):
                h = field[j : j + rows, at]
                g = field[ZERN + j : ZERN + j + rows, at]
                for base, value in ((j, re * h + im * g), (ZERN + j, re * g - im * h)):
                    high = value.astype(BF16)
                    left[base : base + rows, at] = high
                    low = (value - high.astype(F32)).astype(BF16)
                    left[2 * ZERN + base : 2 * ZERN + base + rows, at] = low

    def multiply(left, c, r):
        block = volt_ref[c].reshape(parts * stations, times)
        both = lax.dot_general(block, left[...], NT, preferred_element_type=F32)
        both = both[:, : 2 * ZERN] + both[:, 2 * ZERN :]
        real, imag = both[:stations], pltpu.roll(both[stations:], ZERN, 1)
        out = real + jnp.where(lane < ZERN, -imag, imag)
        part[c, pl.ds(r, stations, stride=REFS), :] = out

    def run(c, first, stop):
        def body(i, carry):
            r = 2 * i
            build(left_b, c, r + 1)
            multiply(left_a, c, r)
            follow = r + 2
            wrap = follow == REFS
            build(left_a, jnp.where(wrap, min(c + 1, chans - 1), c), jnp.where(wrap, 0, follow))
            multiply(left_b, c, r + 1)
            return carry

        lax.fori_loop(first, stop, body, 0)

    own = stations // (n_tm * n_q)
    chunk = own * REFS
    group = chunk * n_q
    order = sorted(range(n_z), key=lambda d: -min(d, n_z - d))

    def block(side_x, dz):
        start = (side_x * n_z + lax.rem(z + dz, n_z)) * group
        return pl.ds(pl.multiple_of(start, group), group)

    def send(src, dst, send, recv, peer):
        copy = pltpu.make_async_remote_copy(
            src_ref=src, dst_ref=dst, send_sem=send, recv_sem=recv,
            device_id=peer, device_id_type=MESH,
        )
        copy.start()
        return copy

    over, copies, final = {}, {}, {}

    def swap(c):
        for k, dz in enumerate(order):
            over[c, k] = send(
                part.at[c, block(other, dz)], side.at[c, k], side_send.at[c, k],
                side_recv.at[c, k], partner,
            )

    def forward(c, k):
        dz = order[k]
        over[c, k].wait_recv()
        held[c, k] = part[c, block(x, dz)] + side[c, k]
        if dz:
            copies[c, k] = send(
                held.at[c, k], got.at[c, k], send_sem.at[c, k], recv_sem.at[c, k], along[dz]
            )

    def reduce(c):
        total = held[c, n_z - 1]
        for k in range(n_z - 1):
            copies[c, k].wait_recv()
            total = total + got[c, k]
        summed[c] = total
        for d in range(1, n_q):
            aim = pl.multiple_of(lax.rem(q + d, n_q) * chunk, chunk)
            final[c, d] = send(
                summed.at[c, pl.ds(aim, chunk)], last.at[c, d - 1], last_send.at[c, d - 1],
                last_recv.at[c, d - 1], across[d],
            )

    def place(c, d, rows):
        origin = lax.rem(q - d + n_q, n_q)
        at = pl.ds(pl.multiple_of((origin * chans + c) * REFS, REFS), REFS)
        for s in range(own):
            out_ref[s, at] = rows[s * REFS : (s + 1) * REFS]

    build(left_a, 0, 0)
    for load in loads:
        load.wait()
    run(0, 0, REFS // 2)
    pl.semaphore_wait(barrier, len(peers))
    swap(0)
    run(1, 0, REFS // 4)
    forward(0, 0)
    run(1, REFS // 4, REFS // 2)
    swap(1)
    for k in range(1, n_z):
        forward(0, k)
    for k in range(n_z - 2):
        forward(1, k)
    reduce(0)
    for k in range(n_z - 2, n_z):
        forward(1, k)
    reduce(1)
    for c in range(chans):
        place(c, 0, summed[c, pl.ds(pl.multiple_of(q * chunk, chunk), chunk)])
    for (c, d), copy in final.items():
        copy.wait_recv()
        place(c, d, last[c, d - 1])
    for copy in (*over.values(), *copies.values(), *final.values()):
        copy.wait_send()


def on_device(voltages, ref_index, positions, aperture_weight):
    chans, parts, stations, times = voltages.shape
    n_stat, n_tm, n_q = lax.axis_size("stat"), lax.axis_size("tm"), lax.axis_size("chan")
    scale = (n_tm * times / CELLS) ** (-0.5)
    zern = jnp.asarray(zernike_table())
    dft = jnp.asarray(dft_table(scale))
    vmem = pl.BlockSpec(memory_space=pltpu.VMEM)
    hbm = pl.BlockSpec(memory_space=pl.ANY)
    dma = pltpu.SemaphoreType.DMA
    refs, table = pl.pallas_call(
        exchange_kernel,
        out_shape=(
            jax.ShapeDtypeStruct((chans, 2 * REFS, times), F32),
            jax.ShapeDtypeStruct((4 * ZERN, CELLS), BF16),
        ),
        in_specs=[hbm, pl.BlockSpec(memory_space=pltpu.SMEM), vmem, vmem, hbm],
        out_specs=(vmem, vmem),
        scratch_shapes=[
            pltpu.VMEM(voltages.shape, BF16),
            pltpu.VMEM(dft.shape, F32),
            pltpu.VMEM((chans, 2 * REFS, times), BF16),
            pltpu.VMEM((n_stat - 1, chans, 2 * REFS, times), BF16),
            pltpu.VMEM((ZERN, 2 * ZERN), F32),
            dma((chans + 1,)),
            dma((n_stat - 1, chans)),
            dma((n_stat - 1, chans)),
        ],
        compiler_params=pltpu.CompilerParams(collective_id=0, has_side_effects=True),
        name="exchange",
    )(voltages, ref_index, zern, aperture_weight[None, :], dft)
    n_z = n_tm // 2
    own = stations // (n_tm * n_q)
    group = n_q * own * REFS
    wide = 2 * ZERN
    out = pl.pallas_call(
        correlate_kernel,
        out_shape=jax.ShapeDtypeStruct((own, n_q * chans * REFS, wide), F32),
        in_specs=[hbm, vmem, vmem, vmem],
        out_specs=vmem,
        scratch_shapes=[
            pltpu.VMEM(voltages.shape, BF16),
            pltpu.VMEM((wide, times), F32),
            pltpu.VMEM((2 * wide, times), BF16),
            pltpu.VMEM((2 * wide, times), BF16),
            pltpu.VMEM((chans, stations * REFS, wide), F32),
            pltpu.VMEM((chans, n_z, group, wide), F32),
            pltpu.VMEM((chans, n_z, group, wide), F32),
            pltpu.VMEM((chans, n_z - 1, group, wide), F32),
            pltpu.VMEM((chans, group, wide), F32),
            pltpu.VMEM((chans, n_q - 1, own * REFS, wide), F32),
            dma((chans, n_z)),
            dma((chans, n_z)),
            dma((chans, n_z - 1)),
            dma((chans, n_z - 1)),
            dma((chans, n_q - 1)),
            dma((chans, n_q - 1)),
            dma((chans,)),
        ],
        compiler_params=pltpu.CompilerParams(collective_id=1, has_side_effects=True),
        name="correlate",
    )(voltages, refs, positions[None, :], table)
    return out.reshape(own, n_q * chans, REFS, 2 * ZERN)


def solution(mesh):
    in_specs = (P("chan", None, "stat", "tm"), P(), P("tm"), P())
    out_specs = P(("stat", "tm", "chan"), None, None, None)
    return jax.shard_map(
        on_device, mesh=mesh, in_specs=in_specs, out_specs=out_specs, check_vma=False
    )
```

```python
import functools
import math

import jax
import jax.numpy as jnp
import numpy as np
from jax import lax
from jax.experimental import pallas as pl
from jax.experimental.pallas import tpu as pltpu
from jax.sharding import PartitionSpec as P

RASTER = 16
CELLS = RASTER * RASTER
ZERN = 64
REFS = 8
MESH = pl.DeviceIdType.MESH
F32 = jnp.float32
BF16 = jnp.bfloat16
HIGHEST = lax.Precision.HIGHEST
NT = (((1,), (1,)), ((), ()))


def zernike_table():
    cells = np.arange(CELLS)
    x = (cells // RASTER - RASTER // 2 + 0.5) / (RASTER / 2.0)
    y = (cells % RASTER - RASTER // 2 + 0.5) / (RASTER / 2.0)
    radius_sq = x * x + y * y
    rows = []
    degree = 0
    while len(rows) < ZERN:
        for azimuth in range(-degree, degree + 1, 2):
            if len(rows) == ZERN:
                break
            order = abs(azimuth)
            power = (x + 1j * y) ** order
            radial = np.zeros_like(x)
            for k in range((degree - order) // 2 + 1):
                weight = (-1) ** k * math.factorial(degree - k)
                weight /= math.factorial(k)
                weight /= math.factorial((degree + order) // 2 - k)
                weight /= math.factorial((degree - order) // 2 - k)
                radial = radial + weight * radius_sq ** ((degree - 2 * k - order) // 2)
            if azimuth > 0:
                row = radial * power.real * math.sqrt(2.0 * (degree + 1))
            elif azimuth < 0:
                row = radial * power.imag * math.sqrt(2.0 * (degree + 1))
            else:
                row = radial * math.sqrt(degree + 1.0)
            rows.append(np.where(radius_sq <= 1.0, row, 0.0))
        degree += 1
    return np.stack(rows).astype(np.float32)


def dft_table(scale):
    cells = np.arange(CELLS)
    a = cells // RASTER - RASTER // 2
    b = cells % RASTER - RASTER // 2
    phases = (a[:, None] * a[None, :] + b[:, None] * b[None, :]) % RASTER
    angles = phases * (2.0 * math.pi / RASTER)
    both = np.concatenate([np.cos(angles), -np.sin(angles)], axis=1)
    return (both * scale).astype(np.float32)


def invert_gram(zern, weight):
    weighted = zern * weight
    gram = lax.dot_general(weighted, zern, NT, precision=HIGHEST, preferred_element_type=F32)
    rows = lax.broadcasted_iota(jnp.int32, (ZERN, ZERN), 0)
    cols = lax.broadcasted_iota(jnp.int32, (ZERN, ZERN), 1)
    both = jnp.concatenate([gram, (rows == cols).astype(F32)], axis=1)
    row_ids = lax.broadcasted_iota(jnp.int32, (ZERN, 2 * ZERN), 0)
    for k in range(ZERN):
        pivot_row = both[k : k + 1, :] * (1.0 / both[k : k + 1, k : k + 1])
        reduced = both - both[:, k : k + 1] * pivot_row
        both = jnp.where(row_ids == k, pivot_row, reduced)
    return weighted, both


def fit_operator(weighted, both, dft):
    padded = jnp.concatenate([jnp.zeros_like(weighted), weighted], axis=0)
    solve = jnp.dot(both, padded, precision=HIGHEST, preferred_element_type=F32)
    return jnp.dot(solve, dft, precision=HIGHEST, preferred_element_type=F32)


def exchange_kernel(
    volt_hbm, index_ref, zern_ref, weight_ref, dft_hbm, out_ref, table_ref,
    volt_ref, dft_ref, own, got, inverse_ref, load_sem, send_sem, recv_sem,
):
    n = lax.axis_size("stat")
    me = lax.axis_index("stat")
    chans, parts, stations, times = volt_ref.shape
    right, left = lax.rem(me + 1, n), lax.rem(me + n - 1, n)
    barrier = pltpu.get_barrier_semaphore()
    for peer in (right, left):
        pl.semaphore_signal(barrier, inc=1, device_id={"stat": peer}, device_id_type=MESH)
    loads = [
        pltpu.make_async_copy(volt_hbm.at[c], volt_ref.at[c], load_sem.at[c])
        for c in range(chans)
    ]
    loads.append(pltpu.make_async_copy(dft_hbm, dft_ref, load_sem.at[chans]))
    for load in loads:
        load.start()
    cols = lax.broadcasted_iota(jnp.int32, (2 * REFS, parts * stations), 1)
    rows = lax.broadcasted_iota(jnp.int32, (2 * REFS, parts * stations), 0)
    wanted = jnp.zeros_like(rows)
    for r in range(REFS):
        wanted = jnp.where(lax.rem(rows, REFS) == r, index_ref[r], wanted)
    wanted = wanted - me * stations
    inside = (wanted >= 0) & (wanted < stations)
    target = jnp.where(inside, wanted, -parts * stations) + (rows // REFS) * stations
    select = jnp.where(cols == target, 1.0, 0.0).astype(BF16)
    for c in range(chans):
        loads[c].wait()
        block = volt_ref[c].reshape(parts * stations, times)
        own[c] = jnp.dot(select, block, preferred_element_type=F32).astype(BF16)
    pl.semaphore_wait(barrier, 2)

    def send(src, slot, c, peer):
        copy = pltpu.make_async_remote_copy(
            src_ref=src, dst_ref=got.at[slot, c], send_sem=send_sem.at[slot, c],
            recv_sem=recv_sem.at[slot, c], device_id={"stat": peer}, device_id_type=MESH,
        )
        copy.start()
        return copy

    copies = {}
    for c in range(chans):
        copies[0, c] = send(own.at[c], 0, c, right)
        copies[1, chans - 1 - c] = send(own.at[chans - 1 - c], 1, chans - 1 - c, left)
    weighted, inverse = invert_gram(zern_ref[...], weight_ref[...])
    inverse_ref[...] = inverse
    copies[0, 0].wait_recv()
    copies[2, 0] = send(got.at[0, 0], 2, 0, right)
    copies[1, 1].wait_recv()
    copies[2, 1] = send(got.at[1, 1], 2, 1, left)
    loads[chans].wait()
    operator = fit_operator(weighted, inverse_ref[...], dft_ref[...])
    table = jnp.concatenate([operator[:, :CELLS], operator[:, CELLS:]], axis=0)
    high = table.astype(BF16)
    table_ref[: 2 * ZERN, :] = high
    table_ref[2 * ZERN :, :] = (table - high.astype(F32)).astype(BF16)
    for slot, c in ((0, 1), (1, 0), (2, 0), (2, 1)):
        copies[slot, c].wait_recv()
    for c in range(chans):
        total = own[c].astype(F32)
        for slot in range(3):
            total = total + got[slot, c].astype(F32)
        out_ref[c] = total
    for copy in copies.values():
        copy.wait_send()


def correlate_kernel(
    volt_hbm, refs_ref, pos_ref, table_ref, out_ref, volt_ref, field, left_a, left_b,
    part, side, held, got, summed, last, side_send, side_recv, send_sem, recv_sem,
    last_send, last_recv, load_sem, cross, joined, cross_send, cross_recv,
):
    tm, q = lax.axis_index("tm"), lax.axis_index("chan")
    n_tm, n_q = lax.axis_size("tm"), lax.axis_size("chan")
    n_z = n_tm // 2
    x, z = tm // n_z, lax.rem(tm, n_z)
    other = 1 - x
    barrier = pltpu.get_barrier_semaphore()
    partner = {"tm": other * n_z + z}
    along = {d: {"tm": x * n_z + lax.rem(z + d, n_z)} for d in range(1, n_z)}
    across = {d: {"chan": lax.rem(q + d, n_q)} for d in range(1, n_q)}
    peers = [partner, *along.values(), *across.values()]
    for peer in peers:
        pl.semaphore_signal(barrier, inc=1, device_id=peer, device_id_type=MESH)
    chans, parts, stations, times = volt_ref.shape
    loads = [
        pltpu.make_async_copy(volt_hbm.at[c], volt_ref.at[c], load_sem.at[c])
        for c in range(chans)
    ]
    for load in loads:
        load.start()
    step = 512
    for t in range(0, times, step):
        cells = lax.broadcasted_iota(jnp.int32, (CELLS, step), 0)
        onehot = jnp.where(cells == pos_ref[:, t : t + step], 1.0, 0.0).astype(BF16)
        both = jnp.dot(table_ref[...], onehot, preferred_element_type=F32)
        field[:, t : t + step] = both[: 2 * ZERN] + both[2 * ZERN :]
    lane = lax.broadcasted_iota(jnp.int32, (stations, 2 * ZERN), 1)
    rows, width = 16, 256

    def build(left, c, r):
        for t in range(0, times, width):
            at = slice(t, t + width)
            re = jnp.broadcast_to(refs_ref[c, pl.ds(r, 1), at], (rows, width))
            im = jnp.broadcast_to(refs_ref[c, pl.ds(r + REFS, 1), at], (rows, width))
            for j in range(0, ZERN, rows):
                h = field[j : j + rows, at]
                g = field[ZERN + j : ZERN + j + rows, at]
                for base, value in ((j, re * h + im * g), (ZERN + j, re * g - im * h)):
                    high = value.astype(BF16)
                    left[base : base + rows, at] = high
                    low = (value - high.astype(F32)).astype(BF16)
                    left[2 * ZERN + base : 2 * ZERN + base + rows, at] = low

    def multiply(left, c, r):
        block = volt_ref[c].reshape(parts * stations, times)
        both = lax.dot_general(block, left[...], NT, preferred_element_type=F32)
        both = both[:, : 2 * ZERN] + both[:, 2 * ZERN :]
        real, imag = both[:stations], pltpu.roll(both[stations:], ZERN, 1)
        out = real + jnp.where(lane < ZERN, -imag, imag)
        part[c, pl.ds(r, stations, stride=REFS), :] = out

    def run(c, first, stop):
        def body(i, carry):
            r = 2 * i
            build(left_b, c, r + 1)
            multiply(left_a, c, r)
            follow = r + 2
            wrap = follow == REFS
            build(left_a, jnp.where(wrap, min(c + 1, chans - 1), c), jnp.where(wrap, 0, follow))
            multiply(left_b, c, r + 1)
            return carry

        lax.fori_loop(first, stop, body, 0)

    own = stations // (n_tm * n_q)
    chunk = own * REFS
    group = chunk * n_q
    order = sorted(range(n_z), key=lambda d: -min(d, n_z - d))

    def block(side_x, dz):
        start = (side_x * n_z + lax.rem(z + dz, n_z)) * group
        return pl.ds(pl.multiple_of(start, group), group)

    def send(src, dst, send, recv, peer):
        copy = pltpu.make_async_remote_copy(
            src_ref=src, dst_ref=dst, send_sem=send, recv_sem=recv,
            device_id=peer, device_id_type=MESH,
        )
        copy.start()
        return copy

    near = ((1, n_z - 1, 2, n_z - 2), (1, n_z - 1))
    rest = [[k for k, d in enumerate(order) if d and d not in near[c]] for c in range(chans)]
    home = n_z - 1
    over, copies, final, crossed = {}, {}, {}, {}

    def swap(c):
        for k in rest[c]:
            over[c, k] = send(
                part.at[c, block(other, order[k])], side.at[c, k], side_send.at[c, k],
                side_recv.at[c, k], partner,
            )
        for i, d in enumerate(near[c]):
            k = order.index(d)
            crossed[c, i] = send(
                part.at[c, block(other, d)], cross.at[c, i], cross_send.at[c, i],
                cross_recv.at[c, i], along[d],
            )
            copies[c, k] = send(
                part.at[c, block(x, d)], got.at[c, k], send_sem.at[c, k], recv_sem.at[c, k],
                along[d],
            )

    def swap_last(c):
        total = part[c, block(other, 0)]
        for i in range(len(near[c])):
            crossed[c, i].wait_recv()
            total = total + cross[c, i]
        joined[c] = total
        over[c, home] = send(
            joined.at[c], side.at[c, home], side_send.at[c, home], side_recv.at[c, home], partner
        )

    def forward(c, k):
        dz = order[k]
        over[c, k].wait_recv()
        held[c, k] = part[c, block(x, dz)] + side[c, k]
        if dz:
            copies[c, k] = send(
                held.at[c, k], got.at[c, k], send_sem.at[c, k], recv_sem.at[c, k], along[dz]
            )

    def reduce(c):
        total = held[c, n_z - 1]
        for k in range(n_z - 1):
            copies[c, k].wait_recv()
            total = total + got[c, k]
        summed[c] = total
        for d in range(1, n_q):
            aim = pl.multiple_of(lax.rem(q + d, n_q) * chunk, chunk)
            final[c, d] = send(
                summed.at[c, pl.ds(aim, chunk)], last.at[c, d - 1], last_send.at[c, d - 1],
                last_recv.at[c, d - 1], across[d],
            )

    def place(c, d, rows):
        origin = lax.rem(q - d + n_q, n_q)
        at = pl.ds(pl.multiple_of((origin * chans + c) * REFS, REFS), REFS)
        for s in range(own):
            out_ref[s, at] = rows[s * REFS : (s + 1) * REFS]

    build(left_a, 0, 0)
    for load in loads:
        load.wait()
    run(0, 0, REFS // 2)
    pl.semaphore_wait(barrier, len(peers))
    swap(0)
    run(1, 0, REFS // 4)
    forward(0, 0)
    run(1, REFS // 4, REFS // 2)
    swap(1)
    swap_last(0)
    for k in rest[0][1:]:
        forward(0, k)
    for k in rest[1][:3]:
        forward(1, k)
    swap_last(1)
    for k in rest[1][3:]:
        forward(1, k)
    forward(0, home)
    reduce(0)
    forward(1, home)
    reduce(1)
    for c in range(chans):
        place(c, 0, summed[c, pl.ds(pl.multiple_of(q * chunk, chunk), chunk)])
    for (c, d), copy in final.items():
        copy.wait_recv()
        place(c, d, last[c, d - 1])
    for copy in (*over.values(), *copies.values(), *crossed.values(), *final.values()):
        copy.wait_send()


def on_device(voltages, ref_index, positions, aperture_weight):
    chans, parts, stations, times = voltages.shape
    n_stat, n_tm, n_q = lax.axis_size("stat"), lax.axis_size("tm"), lax.axis_size("chan")
    scale = (n_tm * times / CELLS) ** (-0.5)
    zern = jnp.asarray(zernike_table())
    dft = jnp.asarray(dft_table(scale))
    vmem = pl.BlockSpec(memory_space=pltpu.VMEM)
    hbm = pl.BlockSpec(memory_space=pl.ANY)
    dma = pltpu.SemaphoreType.DMA
    refs, table = pl.pallas_call(
        exchange_kernel,
        out_shape=(
            jax.ShapeDtypeStruct((chans, 2 * REFS, times), F32),
            jax.ShapeDtypeStruct((4 * ZERN, CELLS), BF16),
        ),
        in_specs=[hbm, pl.BlockSpec(memory_space=pltpu.SMEM), vmem, vmem, hbm],
        out_specs=(vmem, vmem),
        scratch_shapes=[
            pltpu.VMEM(voltages.shape, BF16),
            pltpu.VMEM(dft.shape, F32),
            pltpu.VMEM((chans, 2 * REFS, times), BF16),
            pltpu.VMEM((n_stat - 1, chans, 2 * REFS, times), BF16),
            pltpu.VMEM((ZERN, 2 * ZERN), F32),
            dma((chans + 1,)),
            dma((n_stat - 1, chans)),
            dma((n_stat - 1, chans)),
        ],
        compiler_params=pltpu.CompilerParams(collective_id=0, has_side_effects=True),
        name="exchange",
    )(voltages, ref_index, zern, aperture_weight[None, :], dft)
    n_z = n_tm // 2
    own = stations // (n_tm * n_q)
    group = n_q * own * REFS
    wide = 2 * ZERN
    out = pl.pallas_call(
        correlate_kernel,
        out_shape=jax.ShapeDtypeStruct((own, n_q * chans * REFS, wide), F32),
        in_specs=[hbm, vmem, vmem, vmem],
        out_specs=vmem,
        scratch_shapes=[
            pltpu.VMEM(voltages.shape, BF16),
            pltpu.VMEM((wide, times), F32),
            pltpu.VMEM((2 * wide, times), BF16),
            pltpu.VMEM((2 * wide, times), BF16),
            pltpu.VMEM((chans, stations * REFS, wide), F32),
            pltpu.VMEM((chans, n_z, group, wide), F32),
            pltpu.VMEM((chans, n_z, group, wide), F32),
            pltpu.VMEM((chans, n_z - 1, group, wide), F32),
            pltpu.VMEM((chans, group, wide), F32),
            pltpu.VMEM((chans, n_q - 1, own * REFS, wide), F32),
            dma((chans, n_z)),
            dma((chans, n_z)),
            dma((chans, n_z - 1)),
            dma((chans, n_z - 1)),
            dma((chans, n_q - 1)),
            dma((chans, n_q - 1)),
            dma((chans,)),
            pltpu.VMEM((chans, 4, group, wide), F32),
            pltpu.VMEM((chans, group, wide), F32),
            dma((chans, 4)),
            dma((chans, 4)),
        ],
        compiler_params=pltpu.CompilerParams(collective_id=1, has_side_effects=True),
        name="correlate",
    )(voltages, refs, positions[None, :], table)
    return out.reshape(own, n_q * chans, REFS, 2 * ZERN)


def solution(mesh):
    in_specs = (P("chan", None, "stat", "tm"), P(), P("tm"), P())
    out_specs = P(("stat", "tm", "chan"), None, None, None)
    return jax.shard_map(
        on_device, mesh=mesh, in_specs=in_specs, out_specs=out_specs, check_vma=False
    )
```

```python
import functools
import math

import jax
import jax.numpy as jnp
import numpy as np
from jax import lax
from jax.experimental import pallas as pl
from jax.experimental.pallas import tpu as pltpu
from jax.sharding import PartitionSpec as P

RASTER = 16
CELLS = RASTER * RASTER
ZERN = 64
REFS = 8
MESH = pl.DeviceIdType.MESH
F32 = jnp.float32
BF16 = jnp.bfloat16
HIGHEST = lax.Precision.HIGHEST
NT = (((1,), (1,)), ((), ()))


def zernike_table():
    cells = np.arange(CELLS)
    x = (cells // RASTER - RASTER // 2 + 0.5) / (RASTER / 2.0)
    y = (cells % RASTER - RASTER // 2 + 0.5) / (RASTER / 2.0)
    radius_sq = x * x + y * y
    rows = []
    degree = 0
    while len(rows) < ZERN:
        for azimuth in range(-degree, degree + 1, 2):
            if len(rows) == ZERN:
                break
            order = abs(azimuth)
            power = (x + 1j * y) ** order
            radial = np.zeros_like(x)
            for k in range((degree - order) // 2 + 1):
                weight = (-1) ** k * math.factorial(degree - k)
                weight /= math.factorial(k)
                weight /= math.factorial((degree + order) // 2 - k)
                weight /= math.factorial((degree - order) // 2 - k)
                radial = radial + weight * radius_sq ** ((degree - 2 * k - order) // 2)
            if azimuth > 0:
                row = radial * power.real * math.sqrt(2.0 * (degree + 1))
            elif azimuth < 0:
                row = radial * power.imag * math.sqrt(2.0 * (degree + 1))
            else:
                row = radial * math.sqrt(degree + 1.0)
            rows.append(np.where(radius_sq <= 1.0, row, 0.0))
        degree += 1
    return np.stack(rows).astype(np.float32)


def dft_table(scale):
    cells = np.arange(CELLS)
    a = cells // RASTER - RASTER // 2
    b = cells % RASTER - RASTER // 2
    phases = (a[:, None] * a[None, :] + b[:, None] * b[None, :]) % RASTER
    angles = phases * (2.0 * math.pi / RASTER)
    both = np.concatenate([np.cos(angles), -np.sin(angles)], axis=1)
    return (both * scale).astype(np.float32)


def invert_gram(zern, weight):
    weighted = zern * weight
    gram = lax.dot_general(weighted, zern, NT, precision=HIGHEST, preferred_element_type=F32)
    rows = lax.broadcasted_iota(jnp.int32, (ZERN, ZERN), 0)
    cols = lax.broadcasted_iota(jnp.int32, (ZERN, ZERN), 1)
    both = jnp.concatenate([gram, (rows == cols).astype(F32)], axis=1)
    row_ids = lax.broadcasted_iota(jnp.int32, (ZERN, 2 * ZERN), 0)
    for k in range(ZERN):
        pivot_row = both[k : k + 1, :] * (1.0 / both[k : k + 1, k : k + 1])
        reduced = both - both[:, k : k + 1] * pivot_row
        both = jnp.where(row_ids == k, pivot_row, reduced)
    return weighted, both


def fit_operator(weighted, both, dft):
    padded = jnp.concatenate([jnp.zeros_like(weighted), weighted], axis=0)
    solve = jnp.dot(both, padded, precision=HIGHEST, preferred_element_type=F32)
    return jnp.dot(solve, dft, precision=HIGHEST, preferred_element_type=F32)


def exchange_kernel(
    volt_hbm, index_ref, zern_ref, weight_ref, dft_hbm, out_ref, table_ref,
    volt_ref, dft_ref, own, got, inverse_ref, load_sem, send_sem, recv_sem,
):
    n = lax.axis_size("stat")
    me = lax.axis_index("stat")
    chans, parts, stations, times = volt_ref.shape
    right, left = lax.rem(me + 1, n), lax.rem(me + n - 1, n)
    barrier = pltpu.get_barrier_semaphore()
    for peer in (right, left):
        pl.semaphore_signal(barrier, inc=1, device_id={"stat": peer}, device_id_type=MESH)
    loads = [
        pltpu.make_async_copy(volt_hbm.at[c], volt_ref.at[c], load_sem.at[c])
        for c in range(chans)
    ]
    loads.append(pltpu.make_async_copy(dft_hbm, dft_ref, load_sem.at[chans]))
    for load in loads:
        load.start()
    cols = lax.broadcasted_iota(jnp.int32, (2 * REFS, parts * stations), 1)
    rows = lax.broadcasted_iota(jnp.int32, (2 * REFS, parts * stations), 0)
    wanted = jnp.zeros_like(rows)
    for r in range(REFS):
        wanted = jnp.where(lax.rem(rows, REFS) == r, index_ref[r], wanted)
    wanted = wanted - me * stations
    inside = (wanted >= 0) & (wanted < stations)
    target = jnp.where(inside, wanted, -parts * stations) + (rows // REFS) * stations
    select = jnp.where(cols == target, 1.0, 0.0).astype(BF16)
    for c in range(chans):
        loads[c].wait()
        block = volt_ref[c].reshape(parts * stations, times)
        own[c] = jnp.dot(select, block, preferred_element_type=F32).astype(BF16)
    pl.semaphore_wait(barrier, 2)

    def send(src, slot, c, peer):
        copy = pltpu.make_async_remote_copy(
            src_ref=src, dst_ref=got.at[slot, c], send_sem=send_sem.at[slot, c],
            recv_sem=recv_sem.at[slot, c], device_id={"stat": peer}, device_id_type=MESH,
        )
        copy.start()
        return copy

    copies = {}
    for c in range(chans):
        copies[0, c] = send(own.at[c], 0, c, right)
        copies[1, chans - 1 - c] = send(own.at[chans - 1 - c], 1, chans - 1 - c, left)
    weighted, inverse = invert_gram(zern_ref[...], weight_ref[...])
    inverse_ref[...] = inverse
    copies[0, 0].wait_recv()
    copies[2, 0] = send(got.at[0, 0], 2, 0, right)
    copies[1, 1].wait_recv()
    copies[2, 1] = send(got.at[1, 1], 2, 1, left)
    loads[chans].wait()
    operator = fit_operator(weighted, inverse_ref[...], dft_ref[...])
    table = jnp.concatenate([operator[:, :CELLS], operator[:, CELLS:]], axis=0)
    high = table.astype(BF16)
    table_ref[: 2 * ZERN, :] = high
    table_ref[2 * ZERN :, :] = (table - high.astype(F32)).astype(BF16)
    for slot, c in ((0, 1), (1, 0), (2, 0), (2, 1)):
        copies[slot, c].wait_recv()
    for c in range(chans):
        total = own[c].astype(F32)
        for slot in range(3):
            total = total + got[slot, c].astype(F32)
        out_ref[c] = total
    for copy in copies.values():
        copy.wait_send()


def correlate_kernel(
    volt_hbm, refs_ref, pos_ref, table_ref, out_ref, volt_ref, field, left_a, left_b,
    part, side, held, got, summed, last, side_send, side_recv, send_sem, recv_sem,
    last_send, last_recv, load_sem, cross, joined, cross_send, cross_recv,
):
    tm, q = lax.axis_index("tm"), lax.axis_index("chan")
    n_tm, n_q = lax.axis_size("tm"), lax.axis_size("chan")
    n_z = n_tm // 2
    x, z = tm // n_z, lax.rem(tm, n_z)
    other = 1 - x
    barrier = pltpu.get_barrier_semaphore()
    partner = {"tm": other * n_z + z}
    along = {d: {"tm": x * n_z + lax.rem(z + d, n_z)} for d in range(1, n_z)}
    across = {d: {"chan": lax.rem(q + d, n_q)} for d in range(1, n_q)}
    peers = [partner, *along.values(), *across.values()]
    for peer in peers:
        pl.semaphore_signal(barrier, inc=1, device_id=peer, device_id_type=MESH)
    chans, parts, stations, times = volt_ref.shape
    loads = [
        pltpu.make_async_copy(volt_hbm.at[c], volt_ref.at[c], load_sem.at[c])
        for c in range(chans)
    ]
    for load in loads:
        load.start()
    step = 512
    for t in range(0, times, step):
        cells = lax.broadcasted_iota(jnp.int32, (CELLS, step), 0)
        onehot = jnp.where(cells == pos_ref[:, t : t + step], 1.0, 0.0).astype(BF16)
        both = jnp.dot(table_ref[...], onehot, preferred_element_type=F32)
        field[:, t : t + step] = both[: 2 * ZERN] + both[2 * ZERN :]
    lane = lax.broadcasted_iota(jnp.int32, (stations, 2 * ZERN), 1)
    rows, width = 16, 256

    def build(left, c, r):
        for t in range(0, times, width):
            at = slice(t, t + width)
            re = jnp.broadcast_to(refs_ref[c, pl.ds(r, 1), at], (rows, width))
            im = jnp.broadcast_to(refs_ref[c, pl.ds(r + REFS, 1), at], (rows, width))
            for j in range(0, ZERN, rows):
                h = field[j : j + rows, at]
                g = field[ZERN + j : ZERN + j + rows, at]
                for base, value in ((j, re * h + im * g), (ZERN + j, re * g - im * h)):
                    high = value.astype(BF16)
                    left[base : base + rows, at] = high
                    low = (value - high.astype(F32)).astype(BF16)
                    left[2 * ZERN + base : 2 * ZERN + base + rows, at] = low

    def multiply(left, c, r):
        block = volt_ref[c].reshape(parts * stations, times)
        both = lax.dot_general(block, left[...], NT, preferred_element_type=F32)
        both = both[:, : 2 * ZERN] + both[:, 2 * ZERN :]
        real, imag = both[:stations], pltpu.roll(both[stations:], ZERN, 1)
        out = real + jnp.where(lane < ZERN, -imag, imag)
        part[c, pl.ds(r, stations, stride=REFS), :] = out

    def run(c, first, stop):
        def body(i, carry):
            r = 2 * i
            build(left_b, c, r + 1)
            multiply(left_a, c, r)
            follow = r + 2
            wrap = follow == REFS
            build(left_a, jnp.where(wrap, min(c + 1, chans - 1), c), jnp.where(wrap, 0, follow))
            multiply(left_b, c, r + 1)
            return carry

        lax.fori_loop(first, stop, body, 0)

    own = stations // (n_tm * n_q)
    chunk = own * REFS
    group = chunk * n_q
    far = n_z // 2
    order = [far, far - 1, 2, far + 1, n_z - 2, 1, n_z - 1, 0]

    def block(side_x, dz):
        start = (side_x * n_z + lax.rem(z + dz, n_z)) * group
        return pl.ds(pl.multiple_of(start, group), group)

    def send(src, dst, send, recv, peer):
        copy = pltpu.make_async_remote_copy(
            src_ref=src, dst_ref=dst, send_sem=send, recv_sem=recv,
            device_id=peer, device_id_type=MESH,
        )
        copy.start()
        return copy

    near = ((1, n_z - 1, 2, n_z - 2), (1, n_z - 1))
    rest = [[k for k, d in enumerate(order) if d and d not in near[c]] for c in range(chans)]
    home = n_z - 1
    over, copies, final, crossed = {}, {}, {}, {}

    def swap(c):
        for k in rest[c]:
            over[c, k] = send(
                part.at[c, block(other, order[k])], side.at[c, k], side_send.at[c, k],
                side_recv.at[c, k], partner,
            )
        for i, d in enumerate(near[c]):
            k = order.index(d)
            crossed[c, i] = send(
                part.at[c, block(other, d)], cross.at[c, i], cross_send.at[c, i],
                cross_recv.at[c, i], along[d],
            )
            copies[c, k] = send(
                part.at[c, block(x, d)], got.at[c, k], send_sem.at[c, k], recv_sem.at[c, k],
                along[d],
            )

    def swap_last(c):
        total = part[c, block(other, 0)]
        for i in range(len(near[c])):
            crossed[c, i].wait_recv()
            total = total + cross[c, i]
        joined[c] = total
        over[c, home] = send(
            joined.at[c], side.at[c, home], side_send.at[c, home], side_recv.at[c, home], partner
        )

    def forward(c, k):
        dz = order[k]
        over[c, k].wait_recv()
        total = part[c, block(x, dz)] + side[c, k]
        if dz == far + 1:
            copies[c, 0].wait_recv()
            total = total + got[c, 0]
        held[c, k] = total
        if dz:
            copies[c, k] = send(
                held.at[c, k], got.at[c, k], send_sem.at[c, k], recv_sem.at[c, k],
                along[n_z - 1 if dz == far else dz],
            )

    def reduce(c):
        total = held[c, n_z - 1]
        for k in range(1, n_z - 1):
            copies[c, k].wait_recv()
            total = total + got[c, k]
        summed[c] = total
        for d in range(1, n_q):
            aim = pl.multiple_of(lax.rem(q + d, n_q) * chunk, chunk)
            final[c, d] = send(
                summed.at[c, pl.ds(aim, chunk)], last.at[c, d - 1], last_send.at[c, d - 1],
                last_recv.at[c, d - 1], across[d],
            )

    def place(c, d, rows):
        origin = lax.rem(q - d + n_q, n_q)
        at = pl.ds(pl.multiple_of((origin * chans + c) * REFS, REFS), REFS)
        for s in range(own):
            out_ref[s, at] = rows[s * REFS : (s + 1) * REFS]

    build(left_a, 0, 0)
    for load in loads:
        load.wait()
    run(0, 0, REFS // 2)
    pl.semaphore_wait(barrier, len(peers))
    swap(0)
    run(1, 0, REFS // 4)
    forward(0, 0)
    run(1, REFS // 4, REFS // 2)
    swap(1)
    swap_last(0)
    for k in rest[0][1:]:
        forward(0, k)
    for k in rest[1][:3]:
        forward(1, k)
    swap_last(1)
    for k in rest[1][3:]:
        forward(1, k)
    forward(0, home)
    reduce(0)
    forward(1, home)
    reduce(1)
    for c in range(chans):
        place(c, 0, summed[c, pl.ds(pl.multiple_of(q * chunk, chunk), chunk)])
    for (c, d), copy in final.items():
        copy.wait_recv()
        place(c, d, last[c, d - 1])
    for copy in (*over.values(), *copies.values(), *crossed.values(), *final.values()):
        copy.wait_send()


def on_device(voltages, ref_index, positions, aperture_weight):
    chans, parts, stations, times = voltages.shape
    n_stat, n_tm, n_q = lax.axis_size("stat"), lax.axis_size("tm"), lax.axis_size("chan")
    scale = (n_tm * times / CELLS) ** (-0.5)
    zern = jnp.asarray(zernike_table())
    dft = jnp.asarray(dft_table(scale))
    vmem = pl.BlockSpec(memory_space=pltpu.VMEM)
    hbm = pl.BlockSpec(memory_space=pl.ANY)
    dma = pltpu.SemaphoreType.DMA
    refs, table = pl.pallas_call(
        exchange_kernel,
        out_shape=(
            jax.ShapeDtypeStruct((chans, 2 * REFS, times), F32),
            jax.ShapeDtypeStruct((4 * ZERN, CELLS), BF16),
        ),
        in_specs=[hbm, pl.BlockSpec(memory_space=pltpu.SMEM), vmem, vmem, hbm],
        out_specs=(vmem, vmem),
        scratch_shapes=[
            pltpu.VMEM(voltages.shape, BF16),
            pltpu.VMEM(dft.shape, F32),
            pltpu.VMEM((chans, 2 * REFS, times), BF16),
            pltpu.VMEM((n_stat - 1, chans, 2 * REFS, times), BF16),
            pltpu.VMEM((ZERN, 2 * ZERN), F32),
            dma((chans + 1,)),
            dma((n_stat - 1, chans)),
            dma((n_stat - 1, chans)),
        ],
        compiler_params=pltpu.CompilerParams(collective_id=0, has_side_effects=True),
        name="exchange",
    )(voltages, ref_index, zern, aperture_weight[None, :], dft)
    n_z = n_tm // 2
    own = stations // (n_tm * n_q)
    group = n_q * own * REFS
    wide = 2 * ZERN
    out = pl.pallas_call(
        correlate_kernel,
        out_shape=jax.ShapeDtypeStruct((own, n_q * chans * REFS, wide), F32),
        in_specs=[hbm, vmem, vmem, vmem],
        out_specs=vmem,
        scratch_shapes=[
            pltpu.VMEM(voltages.shape, BF16),
            pltpu.VMEM((wide, times), F32),
            pltpu.VMEM((2 * wide, times), BF16),
            pltpu.VMEM((2 * wide, times), BF16),
            pltpu.VMEM((chans, stations * REFS, wide), F32),
            pltpu.VMEM((chans, n_z, group, wide), F32),
            pltpu.VMEM((chans, n_z, group, wide), F32),
            pltpu.VMEM((chans, n_z - 1, group, wide), F32),
            pltpu.VMEM((chans, group, wide), F32),
            pltpu.VMEM((chans, n_q - 1, own * REFS, wide), F32),
            dma((chans, n_z)),
            dma((chans, n_z)),
            dma((chans, n_z - 1)),
            dma((chans, n_z - 1)),
            dma((chans, n_q - 1)),
            dma((chans, n_q - 1)),
            dma((chans,)),
            pltpu.VMEM((chans, 4, group, wide), F32),
            pltpu.VMEM((chans, group, wide), F32),
            dma((chans, 4)),
            dma((chans, 4)),
        ],
        compiler_params=pltpu.CompilerParams(collective_id=1, has_side_effects=True),
        name="correlate",
    )(voltages, refs, positions[None, :], table)
    return out.reshape(own, n_q * chans, REFS, 2 * ZERN)


def solution(mesh):
    in_specs = (P("chan", None, "stat", "tm"), P(), P("tm"), P())
    out_specs = P(("stat", "tm", "chan"), None, None, None)
    return jax.shard_map(
        on_device, mesh=mesh, in_specs=in_specs, out_specs=out_specs, check_vma=False
    )
```

```python
import functools
import math

import jax
import jax.numpy as jnp
import numpy as np
from jax import lax
from jax.experimental import pallas as pl
from jax.experimental.pallas import tpu as pltpu
from jax.sharding import PartitionSpec as P

RASTER = 16
CELLS = RASTER * RASTER
ZERN = 64
REFS = 8
MESH = pl.DeviceIdType.MESH
F32 = jnp.float32
BF16 = jnp.bfloat16
HIGHEST = lax.Precision.HIGHEST
NT = (((1,), (1,)), ((), ()))


def zernike_table():
    cells = np.arange(CELLS)
    x = (cells // RASTER - RASTER // 2 + 0.5) / (RASTER / 2.0)
    y = (cells % RASTER - RASTER // 2 + 0.5) / (RASTER / 2.0)
    radius_sq = x * x + y * y
    rows = []
    degree = 0
    while len(rows) < ZERN:
        for azimuth in range(-degree, degree + 1, 2):
            if len(rows) == ZERN:
                break
            order = abs(azimuth)
            power = (x + 1j * y) ** order
            radial = np.zeros_like(x)
            for k in range((degree - order) // 2 + 1):
                weight = (-1) ** k * math.factorial(degree - k)
                weight /= math.factorial(k)
                weight /= math.factorial((degree + order) // 2 - k)
                weight /= math.factorial((degree - order) // 2 - k)
                radial = radial + weight * radius_sq ** ((degree - 2 * k - order) // 2)
            if azimuth > 0:
                row = radial * power.real * math.sqrt(2.0 * (degree + 1))
            elif azimuth < 0:
                row = radial * power.imag * math.sqrt(2.0 * (degree + 1))
            else:
                row = radial * math.sqrt(degree + 1.0)
            rows.append(np.where(radius_sq <= 1.0, row, 0.0))
        degree += 1
    return np.stack(rows).astype(np.float32)


def dft_table(scale):
    cells = np.arange(CELLS)
    a = cells // RASTER - RASTER // 2
    b = cells % RASTER - RASTER // 2
    phases = (a[:, None] * a[None, :] + b[:, None] * b[None, :]) % RASTER
    angles = phases * (2.0 * math.pi / RASTER)
    both = np.concatenate([np.cos(angles), -np.sin(angles)], axis=1)
    return (both * scale).astype(np.float32)


def invert_gram(zern, weight):
    weighted = zern * weight
    gram = lax.dot_general(weighted, zern, NT, precision=HIGHEST, preferred_element_type=F32)
    rows = lax.broadcasted_iota(jnp.int32, (ZERN, ZERN), 0)
    cols = lax.broadcasted_iota(jnp.int32, (ZERN, ZERN), 1)
    both = jnp.concatenate([gram, (rows == cols).astype(F32)], axis=1)
    row_ids = lax.broadcasted_iota(jnp.int32, (ZERN, 2 * ZERN), 0)
    for k in range(ZERN):
        pivot_row = both[k : k + 1, :] * (1.0 / both[k : k + 1, k : k + 1])
        reduced = both - both[:, k : k + 1] * pivot_row
        both = jnp.where(row_ids == k, pivot_row, reduced)
    return weighted, both


def fit_operator(weighted, both, dft):
    padded = jnp.concatenate([jnp.zeros_like(weighted), weighted], axis=0)
    solve = jnp.dot(both, padded, precision=HIGHEST, preferred_element_type=F32)
    return jnp.dot(solve, dft, precision=HIGHEST, preferred_element_type=F32)


def exchange_kernel(
    volt_hbm, index_ref, zern_ref, weight_ref, dft_hbm, out_ref, table_ref,
    volt_ref, dft_ref, own, got, inverse_ref, load_sem, send_sem, recv_sem,
):
    n = lax.axis_size("stat")
    me = lax.axis_index("stat")
    chans, parts, stations, times = volt_ref.shape
    right, left = lax.rem(me + 1, n), lax.rem(me + n - 1, n)
    barrier = pltpu.get_barrier_semaphore()
    for peer in (right, left):
        pl.semaphore_signal(barrier, inc=1, device_id={"stat": peer}, device_id_type=MESH)
    loads = [
        pltpu.make_async_copy(volt_hbm.at[c], volt_ref.at[c], load_sem.at[c])
        for c in range(chans)
    ]
    loads.append(pltpu.make_async_copy(dft_hbm, dft_ref, load_sem.at[chans]))
    for load in loads:
        load.start()
    cols = lax.broadcasted_iota(jnp.int32, (2 * REFS, parts * stations), 1)
    rows = lax.broadcasted_iota(jnp.int32, (2 * REFS, parts * stations), 0)
    wanted = jnp.zeros_like(rows)
    for r in range(REFS):
        wanted = jnp.where(lax.rem(rows, REFS) == r, index_ref[r], wanted)
    wanted = wanted - me * stations
    inside = (wanted >= 0) & (wanted < stations)
    target = jnp.where(inside, wanted, -parts * stations) + (rows // REFS) * stations
    select = jnp.where(cols == target, 1.0, 0.0).astype(BF16)
    for c in range(chans):
        loads[c].wait()
        block = volt_ref[c].reshape(parts * stations, times)
        own[c] = jnp.dot(select, block, preferred_element_type=F32).astype(BF16)
    pl.semaphore_wait(barrier, 2)

    def send(src, slot, c, peer):
        copy = pltpu.make_async_remote_copy(
            src_ref=src, dst_ref=got.at[slot, c], send_sem=send_sem.at[slot, c],
            recv_sem=recv_sem.at[slot, c], device_id={"stat": peer}, device_id_type=MESH,
        )
        copy.start()
        return copy

    copies = {}
    for c in range(chans):
        copies[0, c] = send(own.at[c], 0, c, right)
        copies[1, chans - 1 - c] = send(own.at[chans - 1 - c], 1, chans - 1 - c, left)
    weighted, inverse = invert_gram(zern_ref[...], weight_ref[...])
    inverse_ref[...] = inverse
    copies[0, 0].wait_recv()
    copies[2, 0] = send(got.at[0, 0], 2, 0, right)
    copies[1, 1].wait_recv()
    copies[2, 1] = send(got.at[1, 1], 2, 1, left)
    loads[chans].wait()
    operator = fit_operator(weighted, inverse_ref[...], dft_ref[...])
    table = jnp.concatenate([operator[:, :CELLS], operator[:, CELLS:]], axis=0)
    high = table.astype(BF16)
    table_ref[: 2 * ZERN, :] = high
    table_ref[2 * ZERN :, :] = (table - high.astype(F32)).astype(BF16)
    for slot, c in ((0, 1), (1, 0), (2, 0), (2, 1)):
        copies[slot, c].wait_recv()
    for c in range(chans):
        total = own[c].astype(F32)
        for slot in range(3):
            total = total + got[slot, c].astype(F32)
        out_ref[c] = total
    for copy in copies.values():
        copy.wait_send()


def correlate_kernel(
    volt_hbm, refs_ref, pos_ref, table_ref, out_ref, volt_ref, field, left_a, left_b,
    part, side, held, got, summed, last, side_send, side_recv, send_sem, recv_sem,
    last_send, last_recv, load_sem, cross, joined, cross_send, cross_recv,
):
    tm, q = lax.axis_index("tm"), lax.axis_index("chan")
    n_tm, n_q = lax.axis_size("tm"), lax.axis_size("chan")
    n_z = n_tm // 2
    x, z = tm // n_z, lax.rem(tm, n_z)
    other = 1 - x
    barrier = pltpu.get_barrier_semaphore()
    partner = {"tm": other * n_z + z}
    along = {d: {"tm": x * n_z + lax.rem(z + d, n_z)} for d in range(1, n_z)}
    across = {d: {"chan": lax.rem(q + d, n_q)} for d in range(1, n_q)}
    peers = [partner, *along.values(), *across.values()]
    for peer in peers:
        pl.semaphore_signal(barrier, inc=1, device_id=peer, device_id_type=MESH)
    chans, parts, stations, times = volt_ref.shape
    loads = [
        pltpu.make_async_copy(volt_hbm.at[c], volt_ref.at[c], load_sem.at[c])
        for c in range(chans)
    ]
    for load in loads:
        load.start()
    step = 512
    for t in range(0, times, step):
        cells = lax.broadcasted_iota(jnp.int32, (CELLS, step), 0)
        onehot = jnp.where(cells == pos_ref[:, t : t + step], 1.0, 0.0).astype(BF16)
        both = jnp.dot(table_ref[...], onehot, preferred_element_type=F32)
        field[:, t : t + step] = both[: 2 * ZERN] + both[2 * ZERN :]
    lane = lax.broadcasted_iota(jnp.int32, (stations, 2 * ZERN), 1)
    rows, width = 16, 256

    def build(left, c, r):
        for t in range(0, times, width):
            at = slice(t, t + width)
            re = jnp.broadcast_to(refs_ref[c, pl.ds(r, 1), at], (rows, width))
            im = jnp.broadcast_to(refs_ref[c, pl.ds(r + REFS, 1), at], (rows, width))
            for j in range(0, ZERN, rows):
                h = field[j : j + rows, at]
                g = field[ZERN + j : ZERN + j + rows, at]
                for base, value in ((j, re * h + im * g), (ZERN + j, re * g - im * h)):
                    high = value.astype(BF16)
                    left[base : base + rows, at] = high
                    low = (value - high.astype(F32)).astype(BF16)
                    left[2 * ZERN + base : 2 * ZERN + base + rows, at] = low

    def multiply(left, c, r):
        block = volt_ref[c].reshape(parts * stations, times)
        both = lax.dot_general(block, left[...], NT, preferred_element_type=F32)
        both = both[:, : 2 * ZERN] + both[:, 2 * ZERN :]
        real, imag = both[:stations], pltpu.roll(both[stations:], ZERN, 1)
        out = real + jnp.where(lane < ZERN, -imag, imag)
        part[c, pl.ds(r, stations, stride=REFS), :] = out

    def run(c, first, stop):
        def body(i, carry):
            r = 2 * i
            build(left_b, c, r + 1)
            multiply(left_a, c, r)
            follow = r + 2
            wrap = follow == REFS
            build(left_a, jnp.where(wrap, min(c + 1, chans - 1), c), jnp.where(wrap, 0, follow))
            multiply(left_b, c, r + 1)
            return carry

        lax.fori_loop(first, stop, body, 0)

    own = stations // (n_tm * n_q)
    chunk = own * REFS
    group = chunk * n_q
    order = sorted(range(n_z), key=lambda d: -min(d, n_z - d))

    def block(side_x, dz):
        start = (side_x * n_z + lax.rem(z + dz, n_z)) * group
        return pl.ds(pl.multiple_of(start, group), group)

    def send(src, dst, send, recv, peer):
        copy = pltpu.make_async_remote_copy(
            src_ref=src, dst_ref=dst, send_sem=send, recv_sem=recv,
            device_id=peer, device_id_type=MESH,
        )
        copy.start()
        return copy

    near = ((1, n_z - 1, 2, n_z - 2), (1, n_z - 1))
    rest = [[k for k, d in enumerate(order) if d and d not in near[c]] for c in range(chans)]
    home = n_z - 1
    over, copies, final, crossed = {}, {}, {}, {}

    def swap(c):
        for k in rest[c]:
            over[c, k] = send(
                part.at[c, block(other, order[k])], side.at[c, k], side_send.at[c, k],
                side_recv.at[c, k], partner,
            )
        for i, d in enumerate(near[c]):
            k = order.index(d)
            crossed[c, i] = send(
                part.at[c, block(other, d)], cross.at[c, i], cross_send.at[c, i],
                cross_recv.at[c, i], along[d],
            )
            copies[c, k] = send(
                part.at[c, block(x, d)], got.at[c, k], send_sem.at[c, k], recv_sem.at[c, k],
                along[d],
            )

    def swap_last(c):
        total = part[c, block(other, 0)]
        for i in range(len(near[c])):
            crossed[c, i].wait_recv()
            total = total + cross[c, i]
        joined[c] = total
        over[c, home] = send(
            joined.at[c], side.at[c, home], side_send.at[c, home], side_recv.at[c, home], partner
        )

    def forward(c, k):
        dz = order[k]
        over[c, k].wait_recv()
        held[c, k] = part[c, block(x, dz)] + side[c, k]
        if dz:
            copies[c, k] = send(
                held.at[c, k], got.at[c, k], send_sem.at[c, k], recv_sem.at[c, k], along[dz]
            )

    def reduce(c):
        total = held[c, n_z - 1]
        for k in range(n_z - 1):
            copies[c, k].wait_recv()
            total = total + got[c, k]
        summed[c] = total
        for d in range(1, n_q):
            aim = pl.multiple_of(lax.rem(q + d, n_q) * chunk, chunk)
            final[c, d] = send(
                summed.at[c, pl.ds(aim, chunk)], last.at[c, d - 1], last_send.at[c, d - 1],
                last_recv.at[c, d - 1], across[d],
            )

    def place(c, d, rows):
        origin = lax.rem(q - d + n_q, n_q)
        at = pl.ds(pl.multiple_of((origin * chans + c) * REFS, REFS), REFS)
        for s in range(own):
            out_ref[s, at] = rows[s * REFS : (s + 1) * REFS]

    build(left_a, 0, 0)
    for load in loads:
        load.wait()
    run(0, 0, REFS // 2)
    pl.semaphore_wait(barrier, len(peers))
    swap(0)
    run(1, 0, REFS // 4)
    forward(0, 0)
    run(1, REFS // 4, REFS // 4 + 1)
    forward(0, rest[0][1])
    run(1, REFS // 4 + 1, REFS // 2)
    swap(1)
    swap_last(0)
    for k in rest[0][2:]:
        forward(0, k)
    for k in rest[1][:3]:
        forward(1, k)
    swap_last(1)
    for k in rest[1][3:]:
        forward(1, k)
    forward(0, home)
    reduce(0)
    forward(1, home)
    reduce(1)
    for c in range(chans):
        place(c, 0, summed[c, pl.ds(pl.multiple_of(q * chunk, chunk), chunk)])
    for (c, d), copy in final.items():
        copy.wait_recv()
        place(c, d, last[c, d - 1])
    for copy in (*over.values(), *copies.values(), *crossed.values(), *final.values()):
        copy.wait_send()


def on_device(voltages, ref_index, positions, aperture_weight):
    chans, parts, stations, times = voltages.shape
    n_stat, n_tm, n_q = lax.axis_size("stat"), lax.axis_size("tm"), lax.axis_size("chan")
    scale = (n_tm * times / CELLS) ** (-0.5)
    zern = jnp.asarray(zernike_table())
    dft = jnp.asarray(dft_table(scale))
    vmem = pl.BlockSpec(memory_space=pltpu.VMEM)
    hbm = pl.BlockSpec(memory_space=pl.ANY)
    dma = pltpu.SemaphoreType.DMA
    refs, table = pl.pallas_call(
        exchange_kernel,
        out_shape=(
            jax.ShapeDtypeStruct((chans, 2 * REFS, times), F32),
            jax.ShapeDtypeStruct((4 * ZERN, CELLS), BF16),
        ),
        in_specs=[hbm, pl.BlockSpec(memory_space=pltpu.SMEM), vmem, vmem, hbm],
        out_specs=(vmem, vmem),
        scratch_shapes=[
            pltpu.VMEM(voltages.shape, BF16),
            pltpu.VMEM(dft.shape, F32),
            pltpu.VMEM((chans, 2 * REFS, times), BF16),
            pltpu.VMEM((n_stat - 1, chans, 2 * REFS, times), BF16),
            pltpu.VMEM((ZERN, 2 * ZERN), F32),
            dma((chans + 1,)),
            dma((n_stat - 1, chans)),
            dma((n_stat - 1, chans)),
        ],
        compiler_params=pltpu.CompilerParams(collective_id=0, has_side_effects=True),
        name="exchange",
    )(voltages, ref_index, zern, aperture_weight[None, :], dft)
    n_z = n_tm // 2
    own = stations // (n_tm * n_q)
    group = n_q * own * REFS
    wide = 2 * ZERN
    out = pl.pallas_call(
        correlate_kernel,
        out_shape=jax.ShapeDtypeStruct((own, n_q * chans * REFS, wide), F32),
        in_specs=[hbm, vmem, vmem, vmem],
        out_specs=vmem,
        scratch_shapes=[
            pltpu.VMEM(voltages.shape, BF16),
            pltpu.VMEM((wide, times), F32),
            pltpu.VMEM((2 * wide, times), BF16),
            pltpu.VMEM((2 * wide, times), BF16),
            pltpu.VMEM((chans, stations * REFS, wide), F32),
            pltpu.VMEM((chans, n_z, group, wide), F32),
            pltpu.VMEM((chans, n_z, group, wide), F32),
            pltpu.VMEM((chans, n_z - 1, group, wide), F32),
            pltpu.VMEM((chans, group, wide), F32),
            pltpu.VMEM((chans, n_q - 1, own * REFS, wide), F32),
            dma((chans, n_z)),
            dma((chans, n_z)),
            dma((chans, n_z - 1)),
            dma((chans, n_z - 1)),
            dma((chans, n_q - 1)),
            dma((chans, n_q - 1)),
            dma((chans,)),
            pltpu.VMEM((chans, 4, group, wide), F32),
            pltpu.VMEM((chans, group, wide), F32),
            dma((chans, 4)),
            dma((chans, 4)),
        ],
        compiler_params=pltpu.CompilerParams(collective_id=1, has_side_effects=True),
        name="correlate",
    )(voltages, refs, positions[None, :], table)
    return out.reshape(own, n_q * chans, REFS, 2 * ZERN)


def solution(mesh):
    in_specs = (P("chan", None, "stat", "tm"), P(), P("tm"), P())
    out_specs = P(("stat", "tm", "chan"), None, None, None)
    return jax.shard_map(
        on_device, mesh=mesh, in_specs=in_specs, out_specs=out_specs, check_vma=False
    )
```
